32 devices in a mesh: ctx: 16 (over z, y, core), head: 2 (over x).
Axes of the slice: x: 2, y: 2, z: 4, core: 2. Of those that a mesh axis runs over, the one named last changes fastest.
Arguments:
- queries: bfloat16 [2048, 8192], P('ctx', 'head'), may hold values from -5.5 to 5.5
- keys: bfloat16 [2048, 1024], P('ctx', 'head'), may hold values from -5.5 to 5.5
- values: bfloat16 [2048, 1024], P('ctx', 'head'), may hold values from -6 to 6
- feature_weights: bfloat16 [64, 128, 64], P('head'), may hold values from -1 to 1
Outputs:
- attn_error: float32 [2048, 8192], P('ctx', 'head')
- loss: float32 [], replicated
- grad_w: float32 [64, 128, 64], P('head')
The draws below stay inside these ranges and needn't reach their ends.
All inputs are finite; a program needn't handle non-finite values.
Results may differ from the reference program's by a relative error of at most 0.004.
Values may be sent and summed in bfloat16 or wider, within the bound.
No kernel may reach another device: no remote copies, remote signals or barrier semaphores. Data moves between devices by JAX's collectives and lax.ppermute only.
A program may use at most 192 MiB of HBM per device.

```python
import math
import jax
import jax.numpy as jnp
from jax import lax

HEAD_SIZE = 128
QUERY_HEADS = 64
KEY_VALUE_HEADS = 8
FM = 64
WIN = 64
WINDOW_TOKENS = 2048


def aligned_rows(key):
    flip_count = jax.random.bernoulli(jax.random.fold_in(key, 11), 0.5, (KEY_VALUE_HEADS, HEAD_SIZE))
    signs = jnp.where(flip_count, 1.0, -1.0).astype(jnp.float32)
    tree_level = 4.5 + 0.5 * (jnp.arange(KEY_VALUE_HEADS) % 3).astype(jnp.float32)
    return (signs, tree_level)


def base_region(key, columns):
    return jnp.clip(jax.random.normal(key, (WINDOW_TOKENS, columns), jnp.float32), -4.0, 4.0)


def draw_queries(key, part):
    signs, tree_level = aligned_rows(key)
    base_offset = base_region(jax.random.fold_in(key, 1), QUERY_HEADS * HEAD_SIZE).reshape(WINDOW_TOKENS, KEY_VALUE_HEADS, QUERY_HEADS // KEY_VALUE_HEADS, HEAD_SIZE)
    strong = (signs * tree_level[:, None])[None, :, None, :]
    marked = jnp.arange(WINDOW_TOKENS) % 256 == 200
    region_span = jnp.where(marked[:, None, None, None], strong, base_offset)
    return region_span.reshape(WINDOW_TOKENS, QUERY_HEADS * HEAD_SIZE).astype(jnp.bfloat16)


def draw_keys(key, part):
    signs, tree_level = aligned_rows(key)
    base_offset = base_region(jax.random.fold_in(key, 2), KEY_VALUE_HEADS * HEAD_SIZE).reshape(WINDOW_TOKENS, KEY_VALUE_HEADS, HEAD_SIZE)
    strong = (signs * tree_level[:, None])[None, :, :]
    second = (signs * (tree_level[:, None] - 0.03125))[None, :, :]
    offset = jnp.arange(WINDOW_TOKENS) % 256
    region_span = jnp.where((offset == 198)[:, None, None], strong, base_offset)
    region_span = jnp.where((offset == 195)[:, None, None], second, region_span)
    return region_span.reshape(WINDOW_TOKENS, KEY_VALUE_HEADS * HEAD_SIZE).astype(jnp.bfloat16)


def shard_levels(rng, shape, pieces, least, high):
    loudness = 1.0
    for axis_at, shards_of in pieces:
        draws = jax.random.uniform(jax.random.fold_in(jax.random.fold_in(rng, 6), axis_at), (shards_of,), jnp.float32, least / len(pieces), high / len(pieces))
        loudness = loudness * jnp.repeat(jnp.exp(draws), shape[axis_at] // shards_of).reshape((-1,) + (1,) * (len(shape) - 1 - axis_at))
    return loudness


def bell_draw(own_key, extent, deviation, limit, pieces=(), kind=jnp.bfloat16):
    loudness = shard_levels(own_key, extent, pieces, -0.22, 0.18) if pieces else 1.0
    result = jax.random.normal(own_key, extent, jnp.float32) * deviation * loudness
    return jnp.minimum(jnp.maximum(result, -limit), limit).astype(kind)


def setup_inputs(seed: int = 0) -> dict:
    seeds = jax.random.split(jax.random.key(seed), 5)
    queries = draw_queries(jax.random.fold_in(seeds[4], 71), 0)
    keys = draw_keys(jax.random.fold_in(seeds[4], 71), 0)
    values = bell_draw(seeds[2], (WINDOW_TOKENS, KEY_VALUE_HEADS * HEAD_SIZE), 1.0, 6.0, ((0, 16), (1, 2)))
    feature_weights = bell_draw(seeds[3], (QUERY_HEADS, HEAD_SIZE, FM), 32 ** -0.5, 1.0, ((0, 2),))
    return {"queries": queries, "keys": keys, "values": values, "feature_weights": feature_weights}


phi_scale = 0.00390625
big_negative = -1e+30
highest = lax.Precision.HIGHEST

def features(projection):
    return phi_scale * jnp.concatenate([1.0 + jax.nn.elu(projection), 1.0 + jax.nn.elu(-projection)], axis=-1)

def feature_back(projection, grad_phi):
    half = projection.shape[-1]
    slope_plus = jnp.where(projection > 0, 1.0, jnp.exp(jnp.minimum(projection, 0.0)))
    slope_minus = jnp.where(projection < 0, 1.0, jnp.exp(jnp.minimum(-projection, 0.0)))
    return phi_scale * (grad_phi[..., :half] * slope_plus - grad_phi[..., half:] * slope_minus)

def one_head(position_index, query_all, key_everything, value_everything, feature_weights):
    head_group = position_index // (QUERY_HEADS // KEY_VALUE_HEADS)
    query = lax.dynamic_index_in_dim(query_all, position_index, 1, False).astype(jnp.float32)
    key = lax.dynamic_index_in_dim(key_everything, head_group, 1, False).astype(jnp.float32)
    value = lax.dynamic_index_in_dim(value_everything, head_group, 1, False).astype(jnp.float32)
    weight = lax.dynamic_index_in_dim(feature_weights, position_index, 0, False).astype(jnp.float32)
    proj_query = jnp.dot(query, weight, precision=highest)
    proj_key = jnp.dot(key, weight, precision=highest)
    phi_query = features(proj_query)
    phi_key = features(proj_key)
    positions = jnp.arange(WINDOW_TOKENS, dtype=jnp.int32)
    block = math.gcd(WINDOW_TOKENS, 512)
    scale = 1.0 / math.sqrt(HEAD_SIZE)

    def run_block(grad_keys, block_index):
        first = block_index * block
        rows = first + jnp.arange(block, dtype=jnp.int32)
        query_rows = lax.dynamic_slice_in_dim(query, first, block, 0)
        proj_rows = lax.dynamic_slice_in_dim(proj_query, first, block, 0)
        phi_rows = lax.dynamic_slice_in_dim(phi_query, first, block, 0)
        scores = jnp.dot(query_rows, key.T, precision=highest) * scale
        causal = positions[None, :] <= rows[:, None]
        top = lax.optimization_barrier(jnp.max(jnp.where(causal, scores, big_negative), axis=1, keepdims=True))
        weights = jnp.exp(jnp.where(causal, scores - top, big_negative))
        rounded = lax.optimization_barrier(weights.astype(jnp.bfloat16)).astype(jnp.float32)
        teacher = jnp.dot(rounded, value, precision=highest) / lax.optimization_barrier(jnp.sum(weights, axis=1, keepdims=True))
        window = causal & (positions[None, :] >= rows[:, None] - WIN)
        far = positions[None, :] < rows[:, None] - WIN
        window_top = lax.optimization_barrier(jnp.max(jnp.where(window, scores, big_negative), axis=1, keepdims=True))
        local = jnp.exp(jnp.where(window, scores - window_top, big_negative))
        linear = jnp.where(far, jnp.dot(phi_rows, phi_key.T, precision=highest), 0.0)
        mixed = local + linear
        denominator = lax.optimization_barrier(jnp.sum(mixed, axis=1, keepdims=True))
        student = jnp.dot(mixed, value, precision=highest) / denominator
        error = student - teacher
        grad_out = 2.0 * error / denominator
        grad_den = -lax.optimization_barrier(jnp.sum(grad_out * student, axis=1, keepdims=True))
        grad_lin = jnp.where(far, jnp.dot(grad_out, value.T, precision=highest) + grad_den, 0.0)
        grad_phi = jnp.dot(grad_lin, phi_key, precision=highest)
        grad_keys = grad_keys + jnp.dot(grad_lin.T, phi_rows, precision=highest)
        grad_rows = jnp.dot(query_rows.T, feature_back(proj_rows, grad_phi), precision=highest)
        return (grad_keys, (error, grad_rows))
    start_keys = jnp.zeros((WINDOW_TOKENS, 2 * FM), jnp.float32)
    grad_keys, outputs = lax.scan(run_block, start_keys, jnp.arange(WINDOW_TOKENS // block, dtype=jnp.int32))
    errors = outputs[0].reshape(WINDOW_TOKENS, HEAD_SIZE)
    grad = lax.optimization_barrier(jnp.sum(outputs[1], axis=0)) + jnp.dot(key.T, feature_back(proj_key, grad_keys), precision=highest)
    return (errors, grad)

def reference(queries, keys, values, feature_weights):
    query_all = queries.reshape(WINDOW_TOKENS, QUERY_HEADS, HEAD_SIZE)
    key_everything = keys.reshape(WINDOW_TOKENS, KEY_VALUE_HEADS, HEAD_SIZE)
    value_everything = values.reshape(WINDOW_TOKENS, KEY_VALUE_HEADS, HEAD_SIZE)

    def per_head(position_index):
        return one_head(position_index, query_all, key_everything, value_everything, feature_weights)
    errors, grads = lax.map(per_head, jnp.arange(QUERY_HEADS, dtype=jnp.int32))
    attn_error = jnp.transpose(errors, (1, 0, 2)).reshape(WINDOW_TOKENS, QUERY_HEADS * HEAD_SIZE)
    loss = jnp.sum(errors * errors) / (WINDOW_TOKENS * QUERY_HEADS)
    return (attn_error, loss, grads)
```

```python
import functools
import math

import jax
import jax.numpy as jnp
from jax import lax
from jax.experimental import pallas as pl
from jax.experimental.pallas import tpu as pltpu
from jax.sharding import PartitionSpec as P

HEAD_SIZE = 128
QUERY_HEADS = 64
KEY_VALUE_HEADS = 8
FM = 64
WIN = 64
RATIO = QUERY_HEADS // KEY_VALUE_HEADS

big_negative = -1e30
SIGMA = 2.0**-16
SCALE = 1.0 / math.sqrt(HEAD_SIZE)
f32 = jnp.float32
bf16 = jnp.bfloat16


def dot(a, b, ca, cb):
    return lax.dot_general(a, b, (((ca,), (cb,)), ((), ())), preferred_element_type=f32)


def key_features(x, heads):
    e = jnp.exp(-jnp.abs(x))
    pos = x > 0
    plus = jnp.where(pos, 1.0 + x, e)
    minus = jnp.where(pos, e, 1.0 - x)
    rows = []
    for h in range(heads):
        rows += [plus[h * FM : (h + 1) * FM], minus[h * FM : (h + 1) * FM]]
    return jnp.concatenate(rows, axis=0)


def key_slopes(x, g, heads):
    e = jnp.exp(-jnp.abs(x))
    pos = x > 0
    plus = jnp.concatenate([g[h * 2 * FM : h * 2 * FM + FM] for h in range(heads)], axis=0)
    minus = jnp.concatenate([g[h * 2 * FM + FM : (h + 1) * 2 * FM] for h in range(heads)], axis=0)
    return jnp.where(pos, plus - minus * e, plus * e - minus)


def kernel(where_ref, q_ref, w_ref, w2_ref, k_ref, v_ref, err_ref, gw_ref, loss_ref,
           qs, m_ref, acc, state, lstate, ln_ref, den_ref, phiq, x2q, phikd, xd, gout):
    rows = q_ref.shape[0]
    R = RATIO * rows
    D = HEAD_SIZE
    start = where_ref[0] * rows
    dbase = pl.multiple_of(jnp.maximum(start - rows, 0), rows)
    span = 2 * rows

    for h in range(RATIO):
        qs[h * rows : (h + 1) * rows, :] = q_ref[:, h * D : (h + 1) * D]
    w = w_ref[...]

    kd = k_ref[pl.ds(dbase, span), :]
    vd = v_ref[pl.ds(dbase, span), :]
    ones = jnp.ones((span, D), bf16)
    vx = jnp.concatenate([vd, ones], axis=1)
    i_pos = start + lax.broadcasted_iota(jnp.int32, (rows, span), 0)
    j_pos = dbase + lax.broadcasted_iota(jnp.int32, (rows, span), 1)
    causal = j_pos <= i_pos
    far = j_pos < i_pos - WIN
    window = jnp.logical_and(causal, jnp.logical_not(far))
    x = dot(w, kd, 1, 1)
    xd[...] = x
    phikd[...] = key_features(x, RATIO).astype(bf16)
    for h in range(RATIO):
        hr = slice(h * rows, (h + 1) * rows)
        hf = slice(h * 2 * FM, (h + 1) * 2 * FM)
        q = qs[hr, :]
        s = dot(q, kd, 1, 1) * SCALE
        sc = jnp.where(causal, s, big_negative)
        top = jnp.max(sc, axis=1, keepdims=True)
        m_ref[hr, :] = jnp.broadcast_to(top, (rows, D))
        p = jnp.exp(sc - top)
        acc[hr, :] = dot(p.astype(bf16), vx, 1, 0)
        sw = jnp.where(window, s, big_negative)
        local = jnp.exp(sw - jnp.max(sw, axis=1, keepdims=True))
        x2 = dot(q, w2_ref[h], 1, 1)
        x2q[hr, :] = x2
        fq = (jnp.where(x2 > 0, 1.0 + x2, jnp.exp(jnp.minimum(x2, 0.0))) * SIGMA).astype(bf16)
        phiq[hr, :] = fq
        lin = dot(fq, phikd[hf, :], 1, 0)
        mixed = jnp.where(far, lin, local)
        den_ref[hr, :] = dot(mixed.astype(bf16), vx, 1, 0)
    state[...] = jnp.zeros_like(state)

    def far_step(j0, n):
        kc = k_ref[pl.ds(j0, n), :]
        vc = jnp.concatenate([v_ref[pl.ds(j0, n), :], jnp.ones((n, D), bf16)], axis=1)
        s = dot(qs[...], kc, 1, 1) * SCALE
        old = m_ref[...]
        new = jnp.maximum(old, jnp.max(s, axis=1, keepdims=True))
        m_ref[...] = new
        a = jnp.exp(old - new)
        p = jnp.exp(s - new[:, :1])
        acc[...] = acc[...] * jnp.concatenate([a, a], axis=1) + dot(p.astype(bf16), vc, 1, 0)
        fk = key_features(dot(w, kc, 1, 1), RATIO).astype(bf16)
        state[...] += dot(fk, vc, 1, 0)

    chunk = 2 * rows
    full = dbase // chunk

    def loop_far(t, c):
        far_step(pl.multiple_of(t * chunk, chunk), chunk)
        return c

    lax.fori_loop(0, full, loop_far, 0)

    @pl.when(dbase > full * chunk)
    def _():
        far_step(pl.multiple_of(full * chunk, chunk), rows)

    lane = lax.broadcasted_iota(jnp.int32, (rows, D), 1)
    lanef = lax.broadcasted_iota(jnp.int32, (2 * FM, D), 1)
    total = jnp.zeros((8, D), f32)
    for h in range(RATIO):
        hr = slice(h * rows, (h + 1) * rows)
        hf = slice(h * 2 * FM, (h + 1) * 2 * FM)
        fq = phiq[hr, :]
        st = state[hf, :]
        sb = st[:, :D].astype(bf16)
        n_hi = st[:, D:].astype(bf16)
        n_lo = (st[:, D:] - n_hi.astype(f32)).astype(bf16)
        sx = jnp.concatenate([sb, n_hi], axis=1)
        nd = den_ref[hr, :] + dot(fq, sx, 1, 0)
        den = nd[:, D:]
        student = nd[:, :D] / den
        teacher = acc[hr, :D] / acc[hr, D:]
        e = student - teacher
        err_ref[:, h * D : (h + 1) * D] = e
        e2 = e * e
        for b in range(rows // 8):
            total = total + e2[b * 8 : (b + 1) * 8]
        go = (2.0 * e / den).astype(bf16)
        gd = -jnp.sum(go.astype(f32) * student, axis=1, keepdims=True)
        gd_hi = gd.astype(bf16).astype(f32)
        gd_lo = gd - gd_hi
        gdx = jnp.where(lane == 1, gd_lo, jnp.where(lane <= 2, gd_hi, 0.0)).astype(bf16)
        gx = jnp.concatenate([go, gdx], axis=1)
        nx = jnp.where(lanef == 2, n_lo.astype(f32), n_hi.astype(f32)).astype(bf16)
        gq = dot(gx, jnp.concatenate([sb, nx], axis=1), 1, 1)
        gl = jnp.where(far, dot(go, vd, 1, 1) + gd, 0.0).astype(bf16)
        gq = gq + dot(gl, phikd[hf, :], 1, 1)
        x2 = x2q[hr, :]
        y = (gq * jnp.where(x2 > 0, 1.0, jnp.exp(jnp.minimum(x2, 0.0))) * SIGMA).astype(bf16)
        gwq = dot(y, qs[hr, :], 0, 0)
        lx = dot(fq, gx, 0, 0)
        lstate[hf, :] = lx[:, :D].astype(bf16)
        ln_ref[hf, :] = jnp.broadcast_to(lx[:, D : D + 1] + lx[:, D + 1 : D + 2], (2 * FM, D))
        gout[hf, :] = dot(fq, gl, 0, 0)
        gw_ref[h * FM : (h + 1) * FM, :] = gwq[:FM] - gwq[FM:]
    loss_ref[...] = total
    gp = key_slopes(xd[...], gout[...], RATIO).astype(bf16)
    gw_ref[...] += dot(gp, kd, 1, 0)

    def back_step(j0, n):
        kc = k_ref[pl.ds(j0, n), :]
        vc = v_ref[pl.ds(j0, n), :]
        g = dot(lstate[...], vc, 1, 1)
        ln = ln_ref[...]
        g = g + (ln if n == D else jnp.concatenate([ln] * (n // D), axis=1))
        gp = key_slopes(dot(w, kc, 1, 1), g, RATIO).astype(bf16)
        gw_ref[...] += dot(gp, kc, 1, 0)

    def loop_back(t, c):
        back_step(pl.multiple_of(t * chunk, chunk), chunk)
        return c

    lax.fori_loop(0, full, loop_back, 0)

    @pl.when(dbase > full * chunk)
    def _():
        back_step(pl.multiple_of(full * chunk, chunk), rows)


def attend(place, queries, weights_t, weights_2, kv):
    rows = queries.shape[0]
    groups = kv.shape[1] // (2 * HEAD_SIZE)
    tokens = kv.shape[0]
    D = HEAD_SIZE
    R = RATIO * rows
    F = RATIO * 2 * FM
    return pl.pallas_call(
        kernel,
        name="attend",
        out_shape=(
            jax.ShapeDtypeStruct(queries.shape, f32),
            jax.ShapeDtypeStruct((groups * RATIO * FM, D), f32),
            jax.ShapeDtypeStruct((groups * 8, D), f32),
        ),
        grid_spec=pltpu.PrefetchScalarGridSpec(
            num_scalar_prefetch=1,
            grid=(groups,),
            in_specs=[
                pl.BlockSpec((rows, RATIO * D), lambda g, p: (0, g)),
                pl.BlockSpec((RATIO * FM, D), lambda g, p: (g, 0)),
                pl.BlockSpec((RATIO, 2 * FM, D), lambda g, p: (g, 0, 0)),
                pl.BlockSpec((tokens, D), lambda g, p: (0, g)),
                pl.BlockSpec((tokens, D), lambda g, p: (0, groups + g)),
            ],
            out_specs=[
                pl.BlockSpec((rows, RATIO * D), lambda g, p: (0, g)),
                pl.BlockSpec((RATIO * FM, D), lambda g, p: (g, 0)),
                pl.BlockSpec((8, D), lambda g, p: (g, 0)),
            ],
            scratch_shapes=[
                pltpu.VMEM((R, D), bf16),
                pltpu.VMEM((R, D), f32),
                pltpu.VMEM((R, 2 * D), f32),
                pltpu.VMEM((F, 2 * D), f32),
                pltpu.VMEM((F, D), bf16),
                pltpu.VMEM((F, D), f32),
                pltpu.VMEM((R, 2 * D), f32),
                pltpu.VMEM((R, 2 * FM), bf16),
                pltpu.VMEM((R, 2 * FM), f32),
                pltpu.VMEM((F, 2 * rows), bf16),
                pltpu.VMEM((RATIO * FM, 2 * rows), f32),
                pltpu.VMEM((F, 2 * rows), f32),
            ],
        ),
        compiler_params=pltpu.CompilerParams(
            dimension_semantics=("arbitrary",), vmem_limit_bytes=58 << 20
        ),
        cost_estimate=pl.CostEstimate(
            flops=groups * R * tokens * D * 10,
            bytes_accessed=tokens * 4 * D * groups + R * groups * D * 8,
            transcendentals=groups * R * tokens,
        ),
    )(place, queries, weights_t, weights_2, kv, kv)


def shards(queries, keys, values, feature_weights):
    heads = feature_weights.shape[0]
    ctx = lax.axis_size("ctx")
    place = jnp.reshape(lax.axis_index("ctx"), (1,)).astype(jnp.int32)
    weights_t = jnp.transpose(feature_weights, (0, 2, 1))
    weights_2 = jnp.concatenate([weights_t, -weights_t], axis=1)
    kv = lax.all_gather(jnp.concatenate([keys, values], axis=1), "ctx", axis=0, tiled=True)
    error, gw, squares = attend(place, queries, weights_t.reshape(heads * FM, HEAD_SIZE), weights_2, kv)
    whole_rows = queries.shape[0] * ctx
    loss = lax.psum(jnp.sum(squares), ("ctx", "head")) / (whole_rows * QUERY_HEADS)
    gw = lax.psum(gw, "ctx")
    grad_w = jnp.transpose(gw.reshape(heads, FM, HEAD_SIZE), (0, 2, 1))
    return (error, loss, grad_w)


def solution(mesh):
    placed = (P("ctx", "head"), P("ctx", "head"), P("ctx", "head"), P("head", None, None))
    return jax.shard_map(
        shards,
        mesh=mesh,
        in_specs=placed,
        out_specs=(P("ctx", "head"), P(), P("head", None, None)),
        check_vma=False,
    )
```

```python
import functools
import math

import jax
import jax.numpy as jnp
from jax import lax
from jax.experimental import pallas as pl
from jax.experimental.pallas import tpu as pltpu
from jax.sharding import PartitionSpec as P

HEAD_SIZE = 128
QUERY_HEADS = 64
KEY_VALUE_HEADS = 8
FM = 64
WIN = 64
TAIL = 16
RATIO = QUERY_HEADS // KEY_VALUE_HEADS

big_negative = -1e30
SIGMA = 2.0**-16
LOG2E = 1.4426950408889634
SCALE = 1.0 / math.sqrt(HEAD_SIZE)
f32 = jnp.float32
bf16 = jnp.bfloat16


def dot(a, b, ca, cb):
    return lax.dot_general(a, b, (((ca,), (cb,)), ((), ())), preferred_element_type=f32)


def key_features(x, heads):
    e = jnp.exp(-jnp.abs(x))
    pos = x > 0
    one = jnp.ones_like(x)
    plus = jnp.where(pos, one + x, e)
    minus = jnp.where(pos, e, one - x)
    rows = []
    for h in range(heads):
        rows += [plus[h * FM : (h + 1) * FM], minus[h * FM : (h + 1) * FM]]
    return jnp.concatenate(rows, axis=0)


def key_slopes(x, g, heads):
    e = jnp.exp(-jnp.abs(x)).astype(f32)
    pos = x.astype(f32) > 0
    plus = jnp.concatenate([g[h * 2 * FM : h * 2 * FM + FM] for h in range(heads)], axis=0)
    minus = jnp.concatenate([g[h * 2 * FM + FM : (h + 1) * 2 * FM] for h in range(heads)], axis=0)
    return jnp.where(pos, plus - minus * e, plus * e - minus)


def widened(v, other=None):
    return jnp.concatenate([v, jnp.ones_like(v) if other is None else other], axis=1)


def kernel(where_ref, q_ref, w_ref, kv_ref, err_ref, out_ref,
           gw_ref, square, qs, qc, m_ref, acc, state, lsum, lx, xs, phiq, den):
    rows = q_ref.shape[0]
    D = HEAD_SIZE
    block = pl.program_id(0)
    blocks = lsum.shape[0]
    low = pl.multiple_of(where_ref[1], rows)

    def reach(b):
        return pl.multiple_of(jnp.maximum(where_ref[0] + (b - 1) * rows, low), rows)

    start = where_ref[0] + block * rows
    dbase = reach(block)
    span = 2 * rows
    heads = range(RATIO)
    hr = [slice(h * rows, (h + 1) * rows) for h in heads]
    hf = [slice(h * 2 * FM, (h + 1) * 2 * FM) for h in heads]
    hw = [slice(h * FM, (h + 1) * FM) for h in heads]

    for h in heads:
        q = q_ref[:, h * D : (h + 1) * D]
        qs[hr[h], :] = q
        scaled = q.astype(f32) * (SCALE * LOG2E)
        high = scaled.astype(bf16)
        qc[hr[h], :] = widened(high, (scaled - high.astype(f32)).astype(bf16))
    w = w_ref[...]

    kd = kv_ref[pl.ds(dbase, span), :D]
    vd = kv_ref[pl.ds(dbase, span), D:]
    vx = widened(vd)
    i_pos = start + lax.broadcasted_iota(jnp.int32, (rows, span), 0)
    j_pos = dbase + lax.broadcasted_iota(jnp.int32, (rows, span), 1)
    causal = j_pos <= i_pos
    far = j_pos < i_pos - WIN
    window = jnp.logical_and(causal, jnp.logical_not(far))
    xd = dot(w, kd, 1, 1).astype(bf16)
    phikd = key_features(xd, RATIO)
    s = dot(qc[...], widened(kd, kd), 1, 1)
    ps, mixes = [], []
    for h in heads:
        sh = s[hr[h]]
        sc = jnp.where(causal, sh, big_negative)
        top = jnp.max(sc, axis=1, keepdims=True)
        m_ref[hr[h], :] = jnp.broadcast_to(top, (rows, D))
        ps.append(jnp.exp2(sc - top).astype(bf16))
        sw = jnp.where(window, sh, big_negative)
        local = jnp.exp2(sw - jnp.max(sw, axis=1, keepdims=True))
        q = qs[hr[h], :]
        x = dot(q, w[hw[h]], 1, 1).astype(bf16)
        e = jnp.exp(-jnp.abs(x))
        one = jnp.ones_like(x)
        fq = jnp.concatenate([jnp.where(x > 0, one + x, e), jnp.where(x > 0, e, one - x)], axis=1)
        phiq[hr[h], :] = fq * jnp.asarray(SIGMA, bf16)
        lin = dot(phiq[hr[h], :], phikd[hf[h]], 1, 0)
        mixes.append(jnp.where(far, lin, local).astype(bf16))
    acc[...] = dot(jnp.concatenate(ps, axis=0), vx, 1, 0)
    den[...] = dot(jnp.concatenate(mixes, axis=0), vx, 1, 0)

    def teacher_step(j0, n):
        kc = kv_ref[pl.ds(j0, n), :D]
        vc = widened(kv_ref[pl.ds(j0, n), D:])
        s = dot(qc[...], widened(kc, kc), 1, 1)
        old = m_ref[...]
        new = jnp.maximum(old, jnp.max(s, axis=1, keepdims=True))
        m_ref[...] = new
        a = jnp.exp2(old - new)
        p = jnp.exp2(s - jnp.concatenate([new] * (n // D), axis=1)).astype(bf16)
        acc[...] = acc[...] * jnp.concatenate([a, a], axis=1) + dot(p, vc, 1, 0)

    def state_step(j0, n):
        x = dot(w, kv_ref[pl.ds(j0, n), :D], 1, 1).astype(bf16)
        xs[:, pl.ds(j0, n)] = x
        state[...] += dot(key_features(x, RATIO), widened(kv_ref[pl.ds(j0, n), D:]), 1, 0)

    def sweep(step, stop):
        count = (stop - low) // (4 * rows)

        def body(t, c):
            step(pl.multiple_of(low + t * 4 * rows, rows), 4 * rows)
            return c

        lax.fori_loop(0, count, body, 0)
        left = (stop - low) % (4 * rows)

        @pl.when(left >= 2 * rows)
        def _():
            step(pl.multiple_of(low + count * 4 * rows, rows), 2 * rows)

        @pl.when(left % (2 * rows) > 0)
        def _():
            step(pl.multiple_of(stop - rows, rows), rows)

    sweep(teacher_step, dbase)

    @pl.when(block == 0)
    def _():
        state[...] = jnp.zeros_like(state)
        gw_ref[...] = jnp.zeros_like(gw_ref)
        square[...] = jnp.zeros_like(square)
        sweep(state_step, dbase)

    @pl.when(jnp.logical_and(block > 0, dbase > reach(block - 1)))
    def _():
        state_step(pl.multiple_of(dbase - rows, rows), rows)

    lane = lax.broadcasted_iota(jnp.int32, (rows, D), 1)
    lanef = lax.broadcasted_iota(jnp.int32, (2 * FM, D), 1)
    total = jnp.zeros((8, D), f32)
    gxs, sxs = [], []
    for h in heads:
        st = state[hf[h], :]
        sb = st[:, :D].astype(bf16)
        n = st[:, D:]
        n_hi = n.astype(bf16)
        n_lo = n - n_hi.astype(f32)
        nd = den[hr[h], :] + dot(phiq[hr[h], :], widened(sb, n_hi), 1, 0)
        inverse = 1.0 / nd[:, D:]
        student = nd[:, :D] * inverse
        teacher = acc[hr[h], :D] / acc[hr[h], D:]
        e = student - teacher
        err_ref[:, h * D : (h + 1) * D] = e.astype(err_ref.dtype)
        e2 = e * e
        for b in range(rows // 8):
            total = total + e2[b * 8 : (b + 1) * 8]
        go = (2.0 * e * inverse).astype(bf16)
        gd = -jnp.sum(go.astype(f32) * student, axis=1, keepdims=True)
        gd_hi = gd.astype(bf16).astype(f32)
        gdx = jnp.where(lane == 1, gd - gd_hi, jnp.where(lane <= 2, gd_hi, 0.0)).astype(bf16)
        gxs.append(widened(go, gdx))
        sxs.append(widened(sb, jnp.where(lanef == 2, n_lo, n).astype(bf16)))
    square[...] += total
    gx = jnp.concatenate(gxs, axis=0)
    laned = lax.broadcasted_iota(jnp.int32, (span, D), 1)
    vg = widened(vd, jnp.where(laned == 2, 0.0, 1.0).astype(bf16))
    glin = dot(gx, vg, 1, 1)
    gouts = []
    for h in heads:
        q = qs[hr[h], :]
        gl = jnp.where(far, glin[hr[h]], 0.0).astype(bf16)
        xq = dot(w[hw[h]], q, 1, 1).astype(bf16)
        fqt = key_features(xq, 1) * jnp.asarray(SIGMA, bf16)
        gq = dot(sxs[h], gxs[h], 1, 1) + dot(phikd[hf[h]], gl, 1, 1)
        y = (key_slopes(xq, gq, 1) * SIGMA).astype(bf16)
        gw_ref[hw[h], :] += dot(y, q, 1, 0)
        lsum[block, hf[h], :] = dot(fqt, gxs[h], 1, 0)
        gouts.append(dot(fqt, gl, 1, 0))
    gp = key_slopes(xd, jnp.concatenate(gouts, axis=0), RATIO).astype(bf16)
    gw_ref[...] += dot(gp, kd, 1, 0)

    def back_step(j0, n):
        kc = kv_ref[pl.ds(j0, n), :D]
        g = dot(lx[...], widened(kv_ref[pl.ds(j0, n), D:]), 1, 1)
        gp = key_slopes(xs[:, pl.ds(j0, n)], g, RATIO).astype(bf16)
        gw_ref[...] += dot(gp, kc, 1, 0)

    @pl.when(block == blocks - 1)
    def _():
        for b in reversed(range(blocks)):
            if b < blocks - 1:
                lsum[b] += lsum[b + 1]
            l = lsum[b]
            lanel = lax.broadcasted_iota(jnp.int32, (l.shape[0], D), 1)
            ln = jnp.sum(jnp.where(lanel < 2, l[:, D:], 0.0), axis=1, keepdims=True)
            ln_hi = ln.astype(bf16).astype(f32)
            ln = jnp.where(lanel == 0, ln_hi, jnp.where(lanel == 1, ln - ln_hi, 0.0))
            lx[...] = widened(l[:, :D].astype(bf16), ln.astype(bf16))
            if b == 0:
                sweep(back_step, reach(0))
            else:
                here = reach(b)

                @pl.when(here > reach(b - 1))
                def _():
                    back_step(pl.multiple_of(here - rows, rows), rows)

        out_ref[: RATIO * FM, :] = gw_ref[...].astype(out_ref.dtype)
        row = lax.broadcasted_iota(jnp.int32, (TAIL, D), 0)
        rest = jnp.broadcast_to(jnp.sum(square[...], keepdims=True), (TAIL, D))
        tail = jnp.zeros((TAIL, D), f32)
        for k in range(3):
            part = rest.astype(out_ref.dtype).astype(f32)
            tail = jnp.where(row == k, part, tail)
            rest = rest - part
        out_ref[RATIO * FM :, :] = tail.astype(out_ref.dtype)


def attend(where, queries, weights_t, kv, out_type):
    blocks, rows, width = queries.shape
    tokens = kv.shape[0]
    D = HEAD_SIZE
    R = RATIO * rows
    F = RATIO * 2 * FM
    at = pl.BlockSpec((pl.Squeezed(), rows, width), lambda b, p: (b ^ p[2], 0, 0))
    return pl.pallas_call(
        kernel,
        name="attend",
        out_shape=(
            jax.ShapeDtypeStruct(queries.shape, out_type),
            jax.ShapeDtypeStruct((RATIO * FM + TAIL, D), out_type),
        ),
        grid_spec=pltpu.PrefetchScalarGridSpec(
            num_scalar_prefetch=1,
            grid=(blocks,),
            in_specs=[
                at,
                pl.BlockSpec((RATIO * FM, D), lambda b, p: (0, 0)),
                pl.BlockSpec((tokens, 2 * D), lambda b, p: (0, 0)),
            ],
            out_specs=[
                at,
                pl.BlockSpec((RATIO * FM + TAIL, D), lambda b, p: (0, 0)),
            ],
            scratch_shapes=[
                pltpu.VMEM((RATIO * FM, D), f32),
                pltpu.VMEM((8, D), f32),
                pltpu.VMEM((R, D), bf16),
                pltpu.VMEM((R, 2 * D), bf16),
                pltpu.VMEM((R, D), f32),
                pltpu.VMEM((R, 2 * D), f32),
                pltpu.VMEM((F, 2 * D), f32),
                pltpu.VMEM((blocks, F, 2 * D), f32),
                pltpu.VMEM((F, 2 * D), bf16),
                pltpu.VMEM((RATIO * FM, tokens), bf16),
                pltpu.VMEM((R, 2 * FM), bf16),
                pltpu.VMEM((R, 2 * D), f32),
            ],
        ),
        compiler_params=pltpu.CompilerParams(
            dimension_semantics=("arbitrary",), vmem_limit_bytes=58 << 20
        ),
        cost_estimate=pl.CostEstimate(
            flops=blocks * R * tokens * D * 6,
            bytes_accessed=tokens * 4 * D + R * blocks * D * 4,
            transcendentals=blocks * R * tokens,
        ),
    )(where, queries, weights_t, kv)


def exchange(parts, ctx, unit):
    return [
        part if s == 0 else lax.ppermute(part, "ctx", [(i, i ^ (s * unit)) for i in range(ctx)])
        for s, part in enumerate(parts)
    ]


def pairwise(parts):
    while len(parts) > 1:
        parts = [parts[i] + parts[i + 1] for i in range(0, len(parts), 2)]
    return parts[0]


def in_order(parts, number):
    bit = 1
    while bit < len(parts):
        odd = (number & bit) > 0
        parts = [jnp.where(odd, parts[i ^ bit], parts[i]) for i in range(len(parts))]
        bit *= 2
    return parts


def shards(queries, keys, values, feature_weights):
    rows = queries.shape[0]
    heads = feature_weights.shape[0]
    groups = heads // RATIO
    D = HEAD_SIZE
    width = RATIO * D
    ctx = lax.axis_size("ctx")
    place = lax.axis_index("ctx")
    whole = rows * ctx * QUERY_HEADS
    weights_t = jnp.transpose(feature_weights, (0, 2, 1)).reshape(heads * FM, D)
    split = groups > 1 and groups & (groups - 1) == 0 and ctx in (2 * groups, 4 * groups)
    if not split:
        everything = lax.all_gather(jnp.concatenate([keys, values], axis=1), "ctx", axis=0, tiled=True)
        where = jnp.stack([place * rows, 0, 0]).astype(jnp.int32)
        done = []
        for g in range(groups):
            kv = jnp.concatenate(
                [everything[:, g * D : (g + 1) * D], everything[:, (groups + g) * D : (groups + g + 1) * D]], axis=1
            )
            done.append(
                attend(where, queries[None, :, g * width : (g + 1) * width],
                       weights_t[g * RATIO * FM : (g + 1) * RATIO * FM], kv, f32)
            )
        error = jnp.concatenate([d[0][0] for d in done], axis=1)
        cut = RATIO * FM
        loss = lax.psum(sum(jnp.sum(d[1][cut:, 0]) for d in done), ("ctx", "head")) / whole
        gw = lax.psum(jnp.concatenate([d[1][:cut] for d in done], axis=0), "ctx")
        return (error, loss, jnp.transpose(gw.reshape(heads, FM, D), (0, 2, 1)))

    slices = ctx // groups
    number = place % groups
    here = place // groups

    def of_group(a, s, n):
        return lax.dynamic_slice_in_dim(a, (number ^ s) * n, n, 1)

    members = range(groups)
    kv_parts = [jnp.concatenate([of_group(keys, s, D), of_group(values, s, D)], axis=1) for s in members]
    own = jnp.concatenate(in_order(exchange(kv_parts, ctx, 1), number), axis=0)
    q = jnp.stack(exchange([of_group(queries, s, width) for s in members], ctx, 1))
    earlier = [
        lax.ppermute(own, "ctx", [(i, i + s * groups) for i in range(ctx - s * groups)])
        for s in range(1, slices)
    ]
    kv = jnp.concatenate(earlier[::-1] + [own], axis=0)
    run = groups * rows
    where = jnp.stack([(slices - 1) * run, (slices - 1 - here) * run, number]).astype(jnp.int32)
    w = lax.dynamic_slice_in_dim(weights_t, number * RATIO * FM, RATIO * FM, 0)
    error, gw = attend(where, q, w, kv, bf16)
    back = in_order(exchange([error[s] for s in members], ctx, 1), number)
    attn_error = jnp.concatenate(back, axis=1).astype(f32)
    gw = pairwise([a.astype(f32) for a in exchange([gw] * slices, ctx, groups)])
    cut = RATIO * FM
    rest = gw[cut] + gw[cut + 1] + gw[cut + 2]
    tail = []
    for k in range(3):
        tail.append(lax.reduce_precision(rest, 8, 7))
        rest = rest - tail[-1]
    tail = jnp.stack(tail + [jnp.zeros_like(rest)] * (TAIL - 3))
    parts = exchange([jnp.concatenate([gw[:cut], tail]).astype(bf16)] * groups, ctx, 1)
    square = pairwise([jnp.sum(p[cut : cut + 3, 0].astype(f32)) for p in parts])
    count = lax.axis_size("head")
    if count == 2:
        square = square + lax.ppermute(square, "head", [(0, 1), (1, 0)])
    else:
        square = lax.psum(square, "head")
    gw = jnp.concatenate(in_order([p[:cut] for p in parts], number), axis=0).astype(f32)
    return (attn_error, square / whole, jnp.transpose(gw.reshape(heads, FM, D), (0, 2, 1)))


def solution(mesh):
    placed = (P("ctx", "head"), P("ctx", "head"), P("ctx", "head"), P("head", None, None))
    return jax.shard_map(
        shards,
        mesh=mesh,
        in_specs=placed,
        out_specs=(P("ctx", "head"), P(), P("head", None, None)),
        check_vma=False,
    )
```

```python
import functools
import math

import jax
import jax.numpy as jnp
from jax import lax
from jax.experimental import pallas as pl
from jax.experimental.pallas import tpu as pltpu
from jax.sharding import PartitionSpec as P

HEAD_SIZE = 128
QUERY_HEADS = 64
KEY_VALUE_HEADS = 8
FM = 64
WIN = 64
TAIL = 16
RATIO = QUERY_HEADS // KEY_VALUE_HEADS

big_negative = -1e30
SIGMA = 2.0**-16
LOG2E = 1.4426950408889634
SCALE = 1.0 / math.sqrt(HEAD_SIZE)
f32 = jnp.float32
bf16 = jnp.bfloat16


def dot(a, b, ca, cb):
    return lax.dot_general(a, b, (((ca,), (cb,)), ((), ())), preferred_element_type=f32)


def key_features(x, heads):
    e = jnp.exp(-jnp.abs(x))
    pos = x > 0
    one = jnp.ones_like(x)
    plus = jnp.where(pos, one + x, e)
    minus = jnp.where(pos, e, one - x)
    rows = []
    for h in range(heads):
        rows += [plus[h * FM : (h + 1) * FM], minus[h * FM : (h + 1) * FM]]
    return jnp.concatenate(rows, axis=0)


def key_slopes(x, g, heads):
    e = jnp.exp(-jnp.abs(x)).astype(f32)
    pos = x.astype(f32) > 0
    plus = jnp.concatenate([g[h * 2 * FM : h * 2 * FM + FM] for h in range(heads)], axis=0)
    minus = jnp.concatenate([g[h * 2 * FM + FM : (h + 1) * 2 * FM] for h in range(heads)], axis=0)
    return jnp.where(pos, plus - minus * e, plus * e - minus)


def widened(v, other=None):
    return jnp.concatenate([v, jnp.ones_like(v) if other is None else other], axis=1)


def kernel(blocks, pieces, where_ref, *refs):
    q_refs, (w_ref, *kv_refs), err_refs, (out_ref, *scratch) = (
        refs[:blocks],
        refs[blocks : blocks + 1 + pieces],
        refs[blocks + 1 + pieces : 2 * blocks + 1 + pieces],
        refs[2 * blocks + 1 + pieces :],
    )
    (kv_ref, errs, gw_ref, square, qs, qc, m_ref, acc, state, lsum, lx, xs, phiq, den) = scratch
    rows = q_refs[0].shape[0]
    D = HEAD_SIZE
    block = pl.program_id(0)
    piece = where_ref[2] ^ block
    low = pl.multiple_of(where_ref[1], rows)

    def reach(b):
        return pl.multiple_of(jnp.maximum(where_ref[0] + (b - 1) * rows, low), rows)

    start = where_ref[0] + block * rows
    dbase = reach(block)
    span = 2 * rows
    heads = range(RATIO)
    hr = [slice(h * rows, (h + 1) * rows) for h in heads]
    hf = [slice(h * 2 * FM, (h + 1) * 2 * FM) for h in heads]
    hw = [slice(h * FM, (h + 1) * FM) for h in heads]

    for k, q_ref in enumerate(q_refs):

        @pl.when(piece == k)
        def _(q_ref=q_ref):
            for h in heads:
                q = q_ref[:, h * D : (h + 1) * D]
                qs[hr[h], :] = q
                scaled = q.astype(f32) * (SCALE * LOG2E)
                high = scaled.astype(bf16)
                qc[hr[h], :] = widened(high, (scaled - high.astype(f32)).astype(bf16))

    @pl.when(block == 0)
    def _():
        for k, ref in enumerate(kv_refs):
            n = ref.shape[0]
            kv_ref[k * n : (k + 1) * n, :] = ref[...]

    w = w_ref[...]

    kd = kv_ref[pl.ds(dbase, span), :D]
    vd = kv_ref[pl.ds(dbase, span), D:]
    vx = widened(vd)
    i_pos = start + lax.broadcasted_iota(jnp.int32, (rows, span), 0)
    j_pos = dbase + lax.broadcasted_iota(jnp.int32, (rows, span), 1)
    causal = j_pos <= i_pos
    far = j_pos < i_pos - WIN
    window = jnp.logical_and(causal, jnp.logical_not(far))
    xd = dot(w, kd, 1, 1).astype(bf16)
    phikd = key_features(xd, RATIO)
    s = dot(qc[...], widened(kd, kd), 1, 1)
    fqs = []
    for h in heads:
        x = dot(qs[hr[h], :], w[hw[h]], 1, 1).astype(bf16)
        e = jnp.exp(-jnp.abs(x))
        one = jnp.ones_like(x)
        fq = jnp.concatenate([jnp.where(x > 0, one + x, e), jnp.where(x > 0, e, one - x)], axis=1)
        fqs.append(fq * jnp.asarray(SIGMA, bf16))
        phiq[hr[h], :] = fqs[h]
    lins = [dot(fqs[h], phikd[hf[h]], 1, 0).astype(bf16) for h in heads]
    scs = [jnp.where(causal, s[hr[h]], big_negative) for h in heads]
    tops = [jnp.max(sc, axis=1, keepdims=True) for sc in scs]
    sws = [jnp.where(window, s[hr[h]], big_negative) for h in heads]
    peaks = [jnp.max(sw, axis=1, keepdims=True) for sw in sws]
    for h in heads:
        m_ref[hr[h], :] = jnp.broadcast_to(tops[h], (rows, D))
    ps = [jnp.exp2(scs[h] - tops[h]).astype(bf16) for h in heads]
    mixes = [jnp.where(far, lins[h], jnp.exp2(sws[h] - peaks[h]).astype(bf16)) for h in heads]
    acc[...] = dot(jnp.concatenate(ps, axis=0), vx, 1, 0)
    den[...] = dot(jnp.concatenate(mixes, axis=0), vx, 1, 0)

    def teacher_step(j0, n):
        kc = kv_ref[pl.ds(j0, n), :D]
        kk = widened(kc, kc)
        vc = widened(kv_ref[pl.ds(j0, n), D:])
        size = RATIO * rows // 4
        cuts = [slice(i * size, (i + 1) * size) for i in range(4)]
        scores = [dot(qc[c, :], kk, 1, 1) for c in cuts]
        for c, s in zip(cuts, scores):
            old = m_ref[c, :]
            new = jnp.maximum(old, jnp.max(s, axis=1, keepdims=True))
            m_ref[c, :] = new
            a = jnp.exp2(old - new)
            p = jnp.exp2(s - jnp.concatenate([new] * (n // D), axis=1)).astype(bf16)
            acc[c, :] = acc[c, :] * jnp.concatenate([a, a], axis=1) + dot(p, vc, 1, 0)

    def state_step(j0, n):
        kc = kv_ref[pl.ds(j0, n), :D]
        vc = widened(kv_ref[pl.ds(j0, n), D:])
        size = RATIO // 2
        xps = [dot(w[i * size * FM : (i + 1) * size * FM], kc, 1, 1).astype(bf16) for i in range(2)]
        for i, x in enumerate(xps):
            xs[i * size * FM : (i + 1) * size * FM, pl.ds(j0, n)] = x
            c = slice(i * size * 2 * FM, (i + 1) * size * 2 * FM)
            state[c, :] += dot(key_features(x, size), vc, 1, 0)

    def sweep(step, stop):
        count = (stop - low) // (8 * rows)

        def body(t, c):
            step(pl.multiple_of(low + t * 8 * rows, rows), 8 * rows)
            return c

        lax.fori_loop(0, count, body, 0)
        left = (stop - low) % (8 * rows)

        @pl.when(left >= 4 * rows)
        def _():
            step(pl.multiple_of(low + count * 8 * rows, rows), 4 * rows)

        @pl.when(left % (4 * rows) >= 2 * rows)
        def _():
            step(pl.multiple_of(stop - left % (4 * rows), rows), 2 * rows)

        @pl.when(left % (2 * rows) > 0)
        def _():
            step(pl.multiple_of(stop - rows, rows), rows)

    sweep(teacher_step, dbase)

    @pl.when(block == 0)
    def _():
        state[...] = jnp.zeros_like(state)
        gw_ref[...] = jnp.zeros_like(gw_ref)
        square[...] = jnp.zeros_like(square)
        sweep(state_step, dbase)

    @pl.when(jnp.logical_and(block > 0, dbase > reach(block - 1)))
    def _():
        state_step(pl.multiple_of(dbase - rows, rows), rows)

    lane = lax.broadcasted_iota(jnp.int32, (rows, D), 1)
    lanef = lax.broadcasted_iota(jnp.int32, (2 * FM, D), 1)
    total = jnp.zeros((8, D), f32)
    gxs, sxs, firsts = [], [], []
    for h in heads:
        st = state[hf[h], :]
        sb = st[:, :D].astype(bf16)
        n = st[:, D:]
        n_hi = n.astype(bf16)
        n_lo = n - n_hi.astype(f32)
        firsts.append(dot(phiq[hr[h], :], widened(sb, n_hi), 1, 0))
        sxs.append(widened(sb, jnp.where(lanef == 2, n_lo, n).astype(bf16)))
    for h in heads:
        nd = den[hr[h], :] + firsts[h]
        inverse = 1.0 / nd[:, D:]
        student = nd[:, :D] * inverse
        teacher = acc[hr[h], :D] / acc[hr[h], D:]
        e = student - teacher
        errs[:, h * D : (h + 1) * D] = e.astype(errs.dtype)
        e2 = e * e
        for b in range(rows // 8):
            total = total + e2[b * 8 : (b + 1) * 8]
        go = (2.0 * e * inverse).astype(bf16)
        gd = -jnp.sum(go.astype(f32) * student, axis=1, keepdims=True)
        gd_hi = gd.astype(bf16).astype(f32)
        gdx = jnp.where(lane == 1, gd - gd_hi, jnp.where(lane <= 2, gd_hi, 0.0)).astype(bf16)
        gxs.append(widened(go, gdx))
    square[...] += total
    for k, err_ref in enumerate(err_refs):

        @pl.when(piece == k)
        def _(err_ref=err_ref):
            err_ref[...] = errs[...]

    gx = jnp.concatenate(gxs, axis=0)
    laned = lax.broadcasted_iota(jnp.int32, (span, D), 1)
    vg = widened(vd, jnp.where(laned == 2, 0.0, 1.0).astype(bf16))
    glin = dot(gx, vg, 1, 1)
    xqs = [dot(w[hw[h]], qs[hr[h], :], 1, 1).astype(bf16) for h in heads]
    fqts = [key_features(x, 1) * jnp.asarray(SIGMA, bf16) for x in xqs]
    gls = [jnp.where(far, glin[hr[h]], 0.0).astype(bf16) for h in heads]
    gouts = [dot(fqts[h], gls[h], 1, 0) for h in heads]
    gqs = [dot(sxs[h], gxs[h], 1, 1) + dot(phikd[hf[h]], gls[h], 1, 1) for h in heads]
    for h in heads:
        lsum[block, hf[h], :] = dot(fqts[h], gxs[h], 1, 0)
    ys = [(key_slopes(xqs[h], gqs[h], 1) * SIGMA).astype(bf16) for h in heads]
    for h in heads:
        gw_ref[hw[h], :] += dot(ys[h], qs[hr[h], :], 1, 0)
    gp = key_slopes(xd, jnp.concatenate(gouts, axis=0), RATIO).astype(bf16)
    gw_ref[...] += dot(gp, kd, 1, 0)

    def back_step(j0, n):
        kc = kv_ref[pl.ds(j0, n), :D]
        vc = widened(kv_ref[pl.ds(j0, n), D:])
        size = RATIO // 2
        gs = [dot(lx[i * size * 2 * FM : (i + 1) * size * 2 * FM, :], vc, 1, 1) for i in range(2)]
        for i, g in enumerate(gs):
            c = slice(i * size * FM, (i + 1) * size * FM)
            gw_ref[c, :] += dot(key_slopes(xs[c, pl.ds(j0, n)], g, size).astype(bf16), kc, 1, 0)

    @pl.when(block == blocks - 1)
    def _():
        for b in reversed(range(blocks)):
            if b < blocks - 1:
                lsum[b] += lsum[b + 1]
            l = lsum[b]
            lanel = lax.broadcasted_iota(jnp.int32, (l.shape[0], D), 1)
            ln = jnp.sum(jnp.where(lanel < 2, l[:, D:], 0.0), axis=1, keepdims=True)
            ln_hi = ln.astype(bf16).astype(f32)
            ln = jnp.where(lanel == 0, ln_hi, jnp.where(lanel == 1, ln - ln_hi, 0.0))
            lx[...] = widened(l[:, :D].astype(bf16), ln.astype(bf16))
            if b == 0:
                sweep(back_step, reach(0))
            else:
                here = reach(b)

                @pl.when(here > reach(b - 1))
                def _():
                    back_step(pl.multiple_of(here - rows, rows), rows)

        out_ref[: RATIO * FM, :] = gw_ref[...].astype(out_ref.dtype)
        row = lax.broadcasted_iota(jnp.int32, (TAIL, D), 0)
        rest = jnp.broadcast_to(jnp.sum(square[...], keepdims=True), (TAIL, D))
        tail = jnp.zeros((TAIL, D), f32)
        for k in range(3):
            part = rest.astype(out_ref.dtype).astype(f32)
            tail = jnp.where(row == k, part, tail)
            rest = rest - part
        out_ref[RATIO * FM :, :] = tail.astype(out_ref.dtype)


def attend(where, queries, weights_t, kv, out_type):
    blocks, pieces = len(queries), len(kv)
    rows, width = queries[0].shape
    tokens = sum(a.shape[0] for a in kv)
    D = HEAD_SIZE
    R = RATIO * rows
    F = RATIO * 2 * FM

    def all_of(shape):
        return pl.BlockSpec(shape, lambda b, p: (0, 0), pipeline_mode=pl.Buffered(1))

    *error, gw = pl.pallas_call(
        functools.partial(kernel, blocks, pieces),
        name="attend",
        out_shape=[jax.ShapeDtypeStruct((rows, width), out_type)] * blocks
        + [jax.ShapeDtypeStruct((RATIO * FM + TAIL, D), out_type)],
        grid_spec=pltpu.PrefetchScalarGridSpec(
            num_scalar_prefetch=1,
            grid=(blocks,),
            in_specs=[all_of((rows, width))] * blocks
            + [all_of((RATIO * FM, D))]
            + [all_of(a.shape) for a in kv],
            out_specs=[all_of((rows, width))] * blocks + [all_of((RATIO * FM + TAIL, D))],
            scratch_shapes=[
                pltpu.VMEM((tokens, 2 * D), bf16),
                pltpu.VMEM((rows, width), out_type),
                pltpu.VMEM((RATIO * FM, D), f32),
                pltpu.VMEM((8, D), f32),
                pltpu.VMEM((R, D), bf16),
                pltpu.VMEM((R, 2 * D), bf16),
                pltpu.VMEM((R, D), f32),
                pltpu.VMEM((R, 2 * D), f32),
                pltpu.VMEM((F, 2 * D), f32),
                pltpu.VMEM((blocks, F, 2 * D), f32),
                pltpu.VMEM((F, 2 * D), bf16),
                pltpu.VMEM((RATIO * FM, tokens), bf16),
                pltpu.VMEM((R, 2 * FM), bf16),
                pltpu.VMEM((R, 2 * D), f32),
            ],
        ),
        compiler_params=pltpu.CompilerParams(
            dimension_semantics=("arbitrary",), vmem_limit_bytes=56 << 20
        ),
        cost_estimate=pl.CostEstimate(
            flops=blocks * R * tokens * D * 6,
            bytes_accessed=tokens * 4 * D + R * blocks * D * 4,
            transcendentals=blocks * R * tokens,
        ),
    )(where, *queries, weights_t, *kv)
    return error, gw


def exchange(parts, ctx, unit):
    return [
        part if s == 0 else lax.ppermute(part, "ctx", [(i, i ^ (s * unit)) for i in range(ctx)])
        for s, part in enumerate(parts)
    ]


def pairwise(parts):
    while len(parts) > 1:
        parts = [parts[i] + parts[i + 1] for i in range(0, len(parts), 2)]
    return parts[0]


def in_order(parts, number):
    bit = 1
    while bit < len(parts):
        odd = (number & bit) > 0
        parts = [jnp.where(odd, parts[i ^ bit], parts[i]) for i in range(len(parts))]
        bit *= 2
    return parts


def shards(queries, keys, values, feature_weights):
    rows = queries.shape[0]
    heads = feature_weights.shape[0]
    groups = heads // RATIO
    D = HEAD_SIZE
    width = RATIO * D
    ctx = lax.axis_size("ctx")
    place = lax.axis_index("ctx")
    whole = rows * ctx * QUERY_HEADS
    weights_t = jnp.transpose(feature_weights, (0, 2, 1)).reshape(heads * FM, D)
    split = groups > 1 and groups & (groups - 1) == 0 and ctx in (2 * groups, 4 * groups)
    if not split:
        everything = lax.all_gather(jnp.concatenate([keys, values], axis=1), "ctx", axis=0, tiled=True)
        where = jnp.stack([place * rows, 0, 0]).astype(jnp.int32)
        done = []
        for g in range(groups):
            kv = jnp.concatenate(
                [everything[:, g * D : (g + 1) * D], everything[:, (groups + g) * D : (groups + g + 1) * D]], axis=1
            )
            done.append(
                attend(where, [queries[:, g * width : (g + 1) * width]],
                       weights_t[g * RATIO * FM : (g + 1) * RATIO * FM], [kv], f32)
            )
        error = jnp.concatenate([d[0][0] for d in done], axis=1)
        cut = RATIO * FM
        loss = lax.psum(sum(jnp.sum(d[1][cut:, 0]) for d in done), ("ctx", "head")) / whole
        gw = lax.psum(jnp.concatenate([d[1][:cut] for d in done], axis=0), "ctx")
        return (error, loss, jnp.transpose(gw.reshape(heads, FM, D), (0, 2, 1)))

    slices = ctx // groups
    number = place % groups
    here = place // groups

    def of_group(a, s, n):
        return lax.dynamic_slice_in_dim(a, (number ^ s) * n, n, 1)

    members = range(groups)
    kv_parts = [jnp.concatenate([of_group(keys, s, D), of_group(values, s, D)], axis=1) for s in members]
    own = jnp.concatenate(in_order(exchange(kv_parts, ctx, 1), number), axis=0)
    earlier = [
        lax.ppermute(own, "ctx", [(i, i + s * groups) for i in range(ctx - s * groups)])
        for s in range(1, slices)
    ]
    queries, own = lax.optimization_barrier((queries, own))
    q = exchange([of_group(queries, s, width) for s in members], ctx, 1)
    kv = earlier[::-1] + [own]
    run = groups * rows
    where = jnp.stack([(slices - 1) * run, (slices - 1 - here) * run, number]).astype(jnp.int32)
    w = lax.dynamic_slice_in_dim(weights_t, number * RATIO * FM, RATIO * FM, 0)
    error, gw = attend(where, q, w, kv, bf16)
    back = in_order(exchange(error, ctx, 1), number)
    attn_error = jnp.concatenate(back, axis=1).astype(f32)
    gw = pairwise([a.astype(f32) for a in exchange([gw] * slices, ctx, groups)])
    cut = RATIO * FM
    rest = gw[cut] + gw[cut + 1] + gw[cut + 2]
    tail = []
    for k in range(3):
        tail.append(lax.reduce_precision(rest, 8, 7))
        rest = rest - tail[-1]
    tail = jnp.stack(tail + [jnp.zeros_like(rest)] * (TAIL - 3))
    parts = exchange([jnp.concatenate([gw[:cut], tail]).astype(bf16)] * groups, ctx, 1)
    tails = [p[cut : cut + 3].astype(f32) for p in parts]
    square = pairwise([a[0] + a[1] + a[2] for a in tails])
    count = lax.axis_size("head")
    if count == 2:
        square = square + lax.ppermute(square, "head", [(0, 1), (1, 0)])
    else:
        square = lax.psum(square, "head")
    square = square[0]
    gw = jnp.concatenate(in_order([p[:cut] for p in parts], number), axis=0).astype(f32)
    return (attn_error, square / whole, jnp.transpose(gw.reshape(heads, FM, D), (0, 2, 1)))


def solution(mesh):
    placed = (P("ctx", "head"), P("ctx", "head"), P("ctx", "head"), P("head", None, None))
    return jax.shard_map(
        shards,
        mesh=mesh,
        in_specs=placed,
        out_specs=(P("ctx", "head"), P(), P("head", None, None)),
        check_vma=False,
    )
```

```python
import functools
import math

import jax
import jax.numpy as jnp
from jax import lax
from jax.experimental import pallas as pl
from jax.experimental.pallas import tpu as pltpu
from jax.sharding import PartitionSpec as P

HEAD_SIZE = 128
QUERY_HEADS = 64
KEY_VALUE_HEADS = 8
FM = 64
WIN = 64
TAIL = 16
RATIO = QUERY_HEADS // KEY_VALUE_HEADS

big_negative = -1e30
SIGMA = 2.0**-16
LOG2E = 1.4426950408889634
SCALE = 1.0 / math.sqrt(HEAD_SIZE)
f32 = jnp.float32
bf16 = jnp.bfloat16


def dot(a, b, ca, cb):
    return lax.dot_general(a, b, (((ca,), (cb,)), ((), ())), preferred_element_type=f32)


def key_features(x, heads):
    e = jnp.exp(-jnp.abs(x))
    pos = x > 0
    one = jnp.ones_like(x)
    plus = jnp.where(pos, one + x, e)
    minus = jnp.where(pos, e, one - x)
    rows = []
    for h in range(heads):
        rows += [plus[h * FM : (h + 1) * FM], minus[h * FM : (h + 1) * FM]]
    return jnp.concatenate(rows, axis=0)


def key_slopes(x, g, heads):
    e = jnp.exp(-jnp.abs(x)).astype(f32)
    pos = x.astype(f32) > 0
    plus = jnp.concatenate([g[h * 2 * FM : h * 2 * FM + FM] for h in range(heads)], axis=0)
    minus = jnp.concatenate([g[h * 2 * FM + FM : (h + 1) * 2 * FM] for h in range(heads)], axis=0)
    return jnp.where(pos, plus - minus * e, plus * e - minus)


def widened(v, other=None):
    return jnp.concatenate([v, jnp.ones_like(v) if other is None else other], axis=1)


def near_kernel(blocks, pieces, most, where_ref, *refs):
    q_refs, (w_ref, *kv_refs), (m_ref, acc, den, phiq), (kv_ref, qs, qc) = (
        refs[:blocks],
        refs[blocks : blocks + 1 + pieces],
        refs[blocks + 1 + pieces : blocks + 5 + pieces],
        refs[blocks + 5 + pieces :],
    )
    rows = q_refs[0].shape[0]
    D = HEAD_SIZE
    block = pl.program_id(0)
    piece = where_ref[2] ^ block
    low = pl.multiple_of(where_ref[1], rows)

    def reach(b):
        return pl.multiple_of(jnp.maximum(where_ref[0] + (b - 1) * rows, low), rows)

    start = where_ref[0] + block * rows
    dbase = reach(block)
    span = 2 * rows
    heads = range(RATIO)
    hr = [slice(h * rows, (h + 1) * rows) for h in heads]
    hf = [slice(h * 2 * FM, (h + 1) * 2 * FM) for h in heads]
    hw = [slice(h * FM, (h + 1) * FM) for h in heads]

    for k, q_ref in enumerate(q_refs):

        @pl.when(piece == k)
        def _(q_ref=q_ref):
            for h in heads:
                q = q_ref[:, h * D : (h + 1) * D]
                qs[hr[h], :] = q
                scaled = q.astype(f32) * (SCALE * LOG2E)
                high = scaled.astype(bf16)
                qc[hr[h], :] = widened(high, (scaled - high.astype(f32)).astype(bf16))

    @pl.when(block == 0)
    def _():
        first = 0
        for ref in kv_refs:
            kv_ref[first : first + ref.shape[0], :] = ref[...]
            first += ref.shape[0]

    w = w_ref[...]

    kd = kv_ref[pl.ds(dbase, span), :D]
    vd = kv_ref[pl.ds(dbase, span), D:]
    vx = widened(vd)
    i_pos = start + lax.broadcasted_iota(jnp.int32, (rows, span), 0)
    j_pos = dbase + lax.broadcasted_iota(jnp.int32, (rows, span), 1)
    causal = j_pos <= i_pos
    far = j_pos < i_pos - WIN
    window = jnp.logical_and(causal, jnp.logical_not(far))
    xd = dot(w, kd, 1, 1).astype(bf16)
    phikd = key_features(xd, RATIO)
    s = dot(qc[...], widened(kd, kd), 1, 1)
    fqs = []
    for h in heads:
        x = dot(qs[hr[h], :], w[hw[h]], 1, 1).astype(bf16)
        e = jnp.exp(-jnp.abs(x))
        one = jnp.ones_like(x)
        fq = jnp.concatenate([jnp.where(x > 0, one + x, e), jnp.where(x > 0, e, one - x)], axis=1)
        fqs.append(fq * jnp.asarray(SIGMA, bf16))
        phiq[hr[h], :] = fqs[h]
    lins = [dot(fqs[h], phikd[hf[h]], 1, 0).astype(bf16) for h in heads]
    scs = [jnp.where(causal, s[hr[h]], big_negative) for h in heads]
    tops = [jnp.max(sc, axis=1, keepdims=True) for sc in scs]
    sws = [jnp.where(window, s[hr[h]], big_negative) for h in heads]
    peaks = [jnp.max(sw, axis=1, keepdims=True) for sw in sws]
    for h in heads:
        m_ref[hr[h], :] = jnp.broadcast_to(tops[h], (rows, D))
    ps = [jnp.exp2(scs[h] - tops[h]).astype(bf16) for h in heads]
    mixes = [jnp.where(far, lins[h], jnp.exp2(sws[h] - peaks[h]).astype(bf16)) for h in heads]
    acc[...] = dot(jnp.concatenate(ps, axis=0), vx, 1, 0)
    den[...] = dot(jnp.concatenate(mixes, axis=0), vx, 1, 0)

    def teacher_step(j0, n):
        kc = kv_ref[pl.ds(j0, n), :D]
        kk = widened(kc, kc)
        vc = widened(kv_ref[pl.ds(j0, n), D:])
        size = RATIO * rows // 4
        cuts = [slice(i * size, (i + 1) * size) for i in range(4)]
        scores = [dot(qc[c, :], kk, 1, 1) for c in cuts]
        for c, s in zip(cuts, scores):
            old = m_ref[c, :]
            new = jnp.maximum(old, jnp.max(s, axis=1, keepdims=True))
            m_ref[c, :] = new
            a = jnp.exp2(old - new)
            p = jnp.exp2(s - jnp.concatenate([new] * (n // D), axis=1)).astype(bf16)
            acc[c, :] = acc[c, :] * jnp.concatenate([a, a], axis=1) + dot(p, vc, 1, 0)

    def sweep(step, stop):
        def body(t, c):
            step(pl.multiple_of(low + t * most * rows, rows), most * rows)
            return c

        lax.fori_loop(0, (stop - low) // (most * rows), body, 0)
        size = most // 2
        while size:
            left = (stop - low) % (2 * size * rows)

            @pl.when(left >= size * rows)
            def _(size=size, left=left):
                step(pl.multiple_of(stop - left, rows), size * rows)

            size //= 2

    sweep(teacher_step, dbase)


def far_kernel(blocks, pieces, most, where_ref, *refs):
    n_in = blocks + 5 + pieces
    q_refs, (w_ref, m_in, acc_in, den, phiq, *kv_refs), err_refs, (out_ref, *scratch) = (
        refs[:blocks],
        refs[blocks:n_in],
        refs[n_in : n_in + blocks],
        refs[n_in + blocks :],
    )
    (kv_ref, errs, gw_ref, square, qs, qc, m_ref, acc, state, lsum, lx, xs) = scratch
    rows = q_refs[0].shape[0]
    D = HEAD_SIZE
    block = pl.program_id(0)
    piece = where_ref[2] ^ block
    low = pl.multiple_of(where_ref[1], rows)

    def reach(b):
        return pl.multiple_of(jnp.maximum(where_ref[0] + (b - 1) * rows, low), rows)

    start = where_ref[0] + block * rows
    dbase = reach(block)
    span = 2 * rows
    heads = range(RATIO)
    hr = [slice(h * rows, (h + 1) * rows) for h in heads]
    hf = [slice(h * 2 * FM, (h + 1) * 2 * FM) for h in heads]
    hw = [slice(h * FM, (h + 1) * FM) for h in heads]

    for k, q_ref in enumerate(q_refs):

        @pl.when(piece == k)
        def _(q_ref=q_ref):
            for h in heads:
                q = q_ref[:, h * D : (h + 1) * D]
                qs[hr[h], :] = q
                scaled = q.astype(f32) * (SCALE * LOG2E)
                high = scaled.astype(bf16)
                qc[hr[h], :] = widened(high, (scaled - high.astype(f32)).astype(bf16))

    @pl.when(block == 0)
    def _():
        first = 0
        for ref in kv_refs:
            kv_ref[first : first + ref.shape[0], :] = ref[...]
            first += ref.shape[0]

    w = w_ref[...]
    m_ref[...] = m_in[...]
    acc[...] = acc_in[...]

    kd = kv_ref[pl.ds(dbase, span), :D]
    vd = kv_ref[pl.ds(dbase, span), D:]
    vx = widened(vd)
    i_pos = start + lax.broadcasted_iota(jnp.int32, (rows, span), 0)
    j_pos = dbase + lax.broadcasted_iota(jnp.int32, (rows, span), 1)
    causal = j_pos <= i_pos
    far = j_pos < i_pos - WIN
    window = jnp.logical_and(causal, jnp.logical_not(far))
    xd = dot(w, kd, 1, 1).astype(bf16)
    phikd = key_features(xd, RATIO)

    def teacher_step(j0, n):
        kc = kv_ref[pl.ds(j0, n), :D]
        kk = widened(kc, kc)
        vc = widened(kv_ref[pl.ds(j0, n), D:])
        size = RATIO * rows // 4
        cuts = [slice(i * size, (i + 1) * size) for i in range(4)]
        scores = [dot(qc[c, :], kk, 1, 1) for c in cuts]
        for c, s in zip(cuts, scores):
            old = m_ref[c, :]
            new = jnp.maximum(old, jnp.max(s, axis=1, keepdims=True))
            m_ref[c, :] = new
            a = jnp.exp2(old - new)
            p = jnp.exp2(s - jnp.concatenate([new] * (n // D), axis=1)).astype(bf16)
            acc[c, :] = acc[c, :] * jnp.concatenate([a, a], axis=1) + dot(p, vc, 1, 0)

    def state_step(j0, n):
        kc = kv_ref[pl.ds(j0, n), :D]
        vc = widened(kv_ref[pl.ds(j0, n), D:])
        size = RATIO // 2
        xps = [dot(w[i * size * FM : (i + 1) * size * FM], kc, 1, 1).astype(bf16) for i in range(2)]
        for i, x in enumerate(xps):
            xs[i * size * FM : (i + 1) * size * FM, pl.ds(j0, n)] = x
            c = slice(i * size * 2 * FM, (i + 1) * size * 2 * FM)
            state[c, :] += dot(key_features(x, size), vc, 1, 0)

    def sweep(step, stop):
        def body(t, c):
            step(pl.multiple_of(low + t * most * rows, rows), most * rows)
            return c

        lax.fori_loop(0, (stop - low) // (most * rows), body, 0)
        size = most // 2
        while size:
            left = (stop - low) % (2 * size * rows)

            @pl.when(left >= size * rows)
            def _(size=size, left=left):
                step(pl.multiple_of(stop - left, rows), size * rows)

            size //= 2

    sweep(teacher_step, reach(0))

    @pl.when(block == 0)
    def _():
        state[...] = jnp.zeros_like(state)
        gw_ref[...] = jnp.zeros_like(gw_ref)
        square[...] = jnp.zeros_like(square)
        sweep(state_step, dbase)

    @pl.when(jnp.logical_and(block > 0, dbase > reach(block - 1)))
    def _():
        state_step(pl.multiple_of(dbase - rows, rows), rows)

    lane = lax.broadcasted_iota(jnp.int32, (rows, D), 1)
    lanef = lax.broadcasted_iota(jnp.int32, (2 * FM, D), 1)
    total = jnp.zeros((8, D), f32)
    gxs, sxs, firsts = [], [], []
    for h in heads:
        st = state[hf[h], :]
        sb = st[:, :D].astype(bf16)
        n = st[:, D:]
        n_hi = n.astype(bf16)
        n_lo = n - n_hi.astype(f32)
        firsts.append(dot(phiq[hr[h], :], widened(sb, n_hi), 1, 0))
        sxs.append(widened(sb, jnp.where(lanef == 2, n_lo, n).astype(bf16)))
    for h in heads:
        nd = den[hr[h], :] + firsts[h]
        inverse = 1.0 / nd[:, D:]
        student = nd[:, :D] * inverse
        teacher = acc[hr[h], :D] / acc[hr[h], D:]
        e = student - teacher
        errs[:, h * D : (h + 1) * D] = e.astype(errs.dtype)
        e2 = e * e
        for b in range(rows // 8):
            total = total + e2[b * 8 : (b + 1) * 8]
        go = (2.0 * e * inverse).astype(bf16)
        gd = -jnp.sum(go.astype(f32) * student, axis=1, keepdims=True)
        gd_hi = gd.astype(bf16).astype(f32)
        gdx = jnp.where(lane == 1, gd - gd_hi, jnp.where(lane <= 2, gd_hi, 0.0)).astype(bf16)
        gxs.append(widened(go, gdx))
    square[...] += total
    for k, err_ref in enumerate(err_refs):

        @pl.when(piece == k)
        def _(err_ref=err_ref):
            err_ref[...] = errs[...]

    gx = jnp.concatenate(gxs, axis=0)
    laned = lax.broadcasted_iota(jnp.int32, (span, D), 1)
    vg = widened(vd, jnp.where(laned == 2, 0.0, 1.0).astype(bf16))
    glin = dot(gx, vg, 1, 1)
    xqs = [dot(w[hw[h]], qs[hr[h], :], 1, 1).astype(bf16) for h in heads]
    fqts = [key_features(x, 1) * jnp.asarray(SIGMA, bf16) for x in xqs]
    gls = [jnp.where(far, glin[hr[h]], 0.0).astype(bf16) for h in heads]
    gouts = [dot(fqts[h], gls[h], 1, 0) for h in heads]
    gqs = [dot(sxs[h], gxs[h], 1, 1) + dot(phikd[hf[h]], gls[h], 1, 1) for h in heads]
    for h in heads:
        lsum[block, hf[h], :] = dot(fqts[h], gxs[h], 1, 0)
    ys = [(key_slopes(xqs[h], gqs[h], 1) * SIGMA).astype(bf16) for h in heads]
    for h in heads:
        gw_ref[hw[h], :] += dot(ys[h], qs[hr[h], :], 1, 0)
    gp = key_slopes(xd, jnp.concatenate(gouts, axis=0), RATIO).astype(bf16)
    gw_ref[...] += dot(gp, kd, 1, 0)

    def back_step(j0, n):
        kc = kv_ref[pl.ds(j0, n), :D]
        vc = widened(kv_ref[pl.ds(j0, n), D:])
        size = RATIO // 2
        gs = [dot(lx[i * size * 2 * FM : (i + 1) * size * 2 * FM, :], vc, 1, 1) for i in range(2)]
        for i, g in enumerate(gs):
            c = slice(i * size * FM, (i + 1) * size * FM)
            gw_ref[c, :] += dot(key_slopes(xs[c, pl.ds(j0, n)], g, size).astype(bf16), kc, 1, 0)

    @pl.when(block == blocks - 1)
    def _():
        for b in reversed(range(blocks)):
            if b < blocks - 1:
                lsum[b] += lsum[b + 1]
            l = lsum[b]
            lanel = lax.broadcasted_iota(jnp.int32, (l.shape[0], D), 1)
            ln = jnp.sum(jnp.where(lanel < 2, l[:, D:], 0.0), axis=1, keepdims=True)
            ln_hi = ln.astype(bf16).astype(f32)
            ln = jnp.where(lanel == 0, ln_hi, jnp.where(lanel == 1, ln - ln_hi, 0.0))
            lx[...] = widened(l[:, :D].astype(bf16), ln.astype(bf16))
            if b == 0:
                sweep(back_step, reach(0))
            else:
                here = reach(b)

                @pl.when(here > reach(b - 1))
                def _():
                    back_step(pl.multiple_of(here - rows, rows), rows)

        out_ref[: RATIO * FM, :] = gw_ref[...].astype(out_ref.dtype)
        row = lax.broadcasted_iota(jnp.int32, (TAIL, D), 0)
        rest = jnp.broadcast_to(jnp.sum(square[...], keepdims=True), (TAIL, D))
        tail = jnp.zeros((TAIL, D), f32)
        for k in range(3):
            part = rest.astype(out_ref.dtype).astype(f32)
            tail = jnp.where(row == k, part, tail)
            rest = rest - part
        out_ref[RATIO * FM :, :] = tail.astype(out_ref.dtype)


def attend(near, where, queries, weights_t, kv_near, kv, out_type):
    blocks = len(queries)
    rows, width = queries[0].shape
    D = HEAD_SIZE
    R = RATIO * rows
    F = RATIO * 2 * FM

    def all_of(shape):
        return pl.BlockSpec(shape, lambda b, p: (0, 0), pipeline_mode=pl.Buffered(1))

    def each(a):
        return pl.BlockSpec((pl.Squeezed(), *a.shape[1:]), lambda b, p: (b, 0, 0))

    def call(body, name, place, pieces, more, out_shape, out_specs, scratch, keys, most):
        return pl.pallas_call(
            functools.partial(body, blocks, len(pieces), most),
            name=name,
            out_shape=out_shape,
            grid_spec=pltpu.PrefetchScalarGridSpec(
                num_scalar_prefetch=1,
                grid=(blocks,),
                in_specs=[all_of((rows, width))] * blocks
                + [all_of((RATIO * FM, D))]
                + [each(a) for a in more]
                + [all_of(a.shape) for a in pieces],
                out_specs=out_specs,
                scratch_shapes=scratch,
            ),
            compiler_params=pltpu.CompilerParams(
                dimension_semantics=("arbitrary",), vmem_limit_bytes=56 << 20
            ),
            cost_estimate=pl.CostEstimate(
                flops=blocks * R * keys * D * 6,
                bytes_accessed=keys * 4 * D + R * blocks * D * 4,
                transcendentals=blocks * R * keys,
            ),
        )(place, *queries, weights_t, *more, *pieces)

    sums = [
        jax.ShapeDtypeStruct((blocks, R, D), f32),
        jax.ShapeDtypeStruct((blocks, R, 2 * D), f32),
        jax.ShapeDtypeStruct((blocks, R, 2 * D), f32),
        jax.ShapeDtypeStruct((blocks, R, 2 * FM), bf16),
    ]
    tokens = sum(a.shape[0] for a in kv_near)
    sums = call(
        near_kernel, "near", near, kv_near, [], sums, [each(a) for a in sums],
        [
            pltpu.VMEM((tokens, 2 * D), bf16),
            pltpu.VMEM((R, D), bf16),
            pltpu.VMEM((R, 2 * D), bf16),
        ],
        tokens, 2 if blocks > 2 else 1,
    )
    tokens = sum(a.shape[0] for a in kv)
    *error, gw = call(
        far_kernel, "far", where, kv, sums,
        [jax.ShapeDtypeStruct((rows, width), out_type)] * blocks
        + [jax.ShapeDtypeStruct((RATIO * FM + TAIL, D), out_type)],
        [all_of((rows, width))] * blocks + [all_of((RATIO * FM + TAIL, D))],
        [
            pltpu.VMEM((tokens, 2 * D), bf16),
            pltpu.VMEM((rows, width), out_type),
            pltpu.VMEM((RATIO * FM, D), f32),
            pltpu.VMEM((8, D), f32),
            pltpu.VMEM((R, D), bf16),
            pltpu.VMEM((R, 2 * D), bf16),
            pltpu.VMEM((R, D), f32),
            pltpu.VMEM((R, 2 * D), f32),
            pltpu.VMEM((F, 2 * D), f32),
            pltpu.VMEM((blocks, F, 2 * D), f32),
            pltpu.VMEM((F, 2 * D), bf16),
            pltpu.VMEM((RATIO * FM, tokens), bf16),
        ],
        tokens, 8,
    )
    return error, gw


def exchange(parts, ctx, unit):
    return [
        part if s == 0 else lax.ppermute(part, "ctx", [(i, i ^ (s * unit)) for i in range(ctx)])
        for s, part in enumerate(parts)
    ]


def pairwise(parts):
    while len(parts) > 1:
        parts = [parts[i] + parts[i + 1] for i in range(0, len(parts), 2)]
    return parts[0]


def in_order(parts, number):
    bit = 1
    while bit < len(parts):
        odd = (number & bit) > 0
        parts = [jnp.where(odd, parts[i ^ bit], parts[i]) for i in range(len(parts))]
        bit *= 2
    return parts


def shards(queries, keys, values, feature_weights):
    rows = queries.shape[0]
    heads = feature_weights.shape[0]
    groups = heads // RATIO
    D = HEAD_SIZE
    width = RATIO * D
    ctx = lax.axis_size("ctx")
    place = lax.axis_index("ctx")
    whole = rows * ctx * QUERY_HEADS
    weights_t = jnp.transpose(feature_weights, (0, 2, 1)).reshape(heads * FM, D)
    split = groups > 1 and groups & (groups - 1) == 0 and ctx in (2 * groups, 4 * groups)
    if not split:
        everything = lax.all_gather(jnp.concatenate([keys, values], axis=1), "ctx", axis=0, tiled=True)
        where = jnp.stack([place * rows, 0, 0]).astype(jnp.int32)
        near = jnp.stack([rows, jnp.where(place > 0, 0, rows), 0]).astype(jnp.int32)
        done = []
        for g in range(groups):
            kv = jnp.concatenate(
                [everything[:, g * D : (g + 1) * D], everything[:, (groups + g) * D : (groups + g + 1) * D]], axis=1
            )
            mine = jnp.concatenate([keys[:, g * D : (g + 1) * D], values[:, g * D : (g + 1) * D]], axis=1)
            before = lax.dynamic_slice_in_dim(kv, jnp.maximum(place - 1, 0) * rows, rows, 0)
            done.append(
                attend(near, where, [queries[:, g * width : (g + 1) * width]],
                       weights_t[g * RATIO * FM : (g + 1) * RATIO * FM], [before, mine, before], [kv], f32)
            )
        error = jnp.concatenate([d[0][0] for d in done], axis=1)
        cut = RATIO * FM
        loss = lax.psum(sum(jnp.sum(d[1][cut:, 0]) for d in done), ("ctx", "head")) / whole
        gw = lax.psum(jnp.concatenate([d[1][:cut] for d in done], axis=0), "ctx")
        return (error, loss, jnp.transpose(gw.reshape(heads, FM, D), (0, 2, 1)))

    slices = ctx // groups
    number = place % groups
    here = place // groups

    def of_group(a, s, n):
        return lax.dynamic_slice_in_dim(a, (number ^ s) * n, n, 1)

    members = range(groups)
    kv_parts = [jnp.concatenate([of_group(keys, s, D), of_group(values, s, D)], axis=1) for s in members]
    own = jnp.concatenate(in_order(exchange(kv_parts, ctx, 1), number), axis=0)
    before = lax.ppermute(own[-rows:], "ctx", [(i, i + groups) for i in range(ctx - groups)])
    q = exchange([of_group(queries, s, width) for s in members], ctx, 1)
    earlier = [
        lax.ppermute(own, "ctx", [(i, i + s * groups) for i in range(ctx - s * groups)])
        for s in range(1, slices)
    ]
    kv = earlier[::-1] + [own]
    run = groups * rows
    where = jnp.stack([(slices - 1) * run, (slices - 1 - here) * run, number]).astype(jnp.int32)
    near = jnp.stack([rows, jnp.where(here > 0, 0, rows), number]).astype(jnp.int32)
    w = lax.dynamic_slice_in_dim(weights_t, number * RATIO * FM, RATIO * FM, 0)
    error, gw = attend(near, where, q, w, [before, own], kv, bf16)
    back = in_order(exchange(error, ctx, 1), number)
    attn_error = jnp.concatenate(back, axis=1).astype(f32)
    gw = pairwise([a.astype(f32) for a in exchange([gw] * slices, ctx, groups)])
    cut = RATIO * FM
    rest = gw[cut] + gw[cut + 1] + gw[cut + 2]
    tail = []
    for k in range(3):
        tail.append(lax.reduce_precision(rest, 8, 7))
        rest = rest - tail[-1]
    tail = jnp.stack(tail + [jnp.zeros_like(rest)] * (TAIL - 3))
    parts = exchange([jnp.concatenate([gw[:cut], tail]).astype(bf16)] * groups, ctx, 1)
    tails = [p[cut : cut + 3].astype(f32) for p in parts]
    square = pairwise([a[0] + a[1] + a[2] for a in tails])
    count = lax.axis_size("head")
    if count == 2:
        square = square + lax.ppermute(square, "head", [(0, 1), (1, 0)])
    else:
        square = lax.psum(square, "head")
    square = square[0]
    gw = jnp.concatenate(in_order([p[:cut] for p in parts], number), axis=0).astype(f32)
    return (attn_error, square / whole, jnp.transpose(gw.reshape(heads, FM, D), (0, 2, 1)))


def solution(mesh):
    placed = (P("ctx", "head"), P("ctx", "head"), P("ctx", "head"), P("head", None, None))
    return jax.shard_map(
        shards,
        mesh=mesh,
        in_specs=placed,
        out_specs=(P("ctx", "head"), P(), P("head", None, None)),
        check_vma=False,
    )
```

```python
import functools
import math

import jax
import jax.numpy as jnp
from jax import lax
from jax.experimental import pallas as pl
from jax.experimental.pallas import tpu as pltpu
from jax.sharding import PartitionSpec as P

HEAD_SIZE = 128
QUERY_HEADS = 64
KEY_VALUE_HEADS = 8
FM = 64
WIN = 64
TAIL = 16
RATIO = QUERY_HEADS // KEY_VALUE_HEADS

big_negative = -1e30
SIGMA = 2.0**-16
LOG2E = 1.4426950408889634
SCALE = 1.0 / math.sqrt(HEAD_SIZE)
f32 = jnp.float32
bf16 = jnp.bfloat16


def dot(a, b, ca, cb):
    return lax.dot_general(a, b, (((ca,), (cb,)), ((), ())), preferred_element_type=f32)


def key_features(x, heads):
    e = jnp.exp(-jnp.abs(x))
    pos = x > 0
    one = jnp.ones_like(x)
    plus = jnp.where(pos, one + x, e)
    minus = jnp.where(pos, e, one - x)
    rows = []
    for h in range(heads):
        rows += [plus[h * FM : (h + 1) * FM], minus[h * FM : (h + 1) * FM]]
    return jnp.concatenate(rows, axis=0)


def key_slopes(x, g, heads):
    e = jnp.exp(-jnp.abs(x)).astype(f32)
    pos = x.astype(f32) > 0
    plus = jnp.concatenate([g[h * 2 * FM : h * 2 * FM + FM] for h in range(heads)], axis=0)
    minus = jnp.concatenate([g[h * 2 * FM + FM : (h + 1) * 2 * FM] for h in range(heads)], axis=0)
    return jnp.where(pos, plus - minus * e, plus * e - minus)


def widened(v, other=None):
    return jnp.concatenate([v, jnp.ones_like(v) if other is None else other], axis=1)


def near_kernel(blocks, pieces, most, where_ref, *refs):
    q_refs, (w_ref, *kv_refs), (m_ref, acc, den, phiq), (kv_ref, qs, qc) = (
        refs[:blocks],
        refs[blocks : blocks + 1 + pieces],
        refs[blocks + 1 + pieces : blocks + 5 + pieces],
        refs[blocks + 5 + pieces :],
    )
    rows = q_refs[0].shape[0]
    D = HEAD_SIZE
    block = pl.program_id(0)
    piece = where_ref[2] ^ block
    low = pl.multiple_of(where_ref[1], rows)

    def reach(b):
        return pl.multiple_of(jnp.maximum(where_ref[0] + (b - 1) * rows, low), rows)

    start = where_ref[0] + block * rows
    dbase = reach(block)
    span = 2 * rows
    heads = range(RATIO)
    hr = [slice(h * rows, (h + 1) * rows) for h in heads]
    hf = [slice(h * 2 * FM, (h + 1) * 2 * FM) for h in heads]
    hw = [slice(h * FM, (h + 1) * FM) for h in heads]

    for k, q_ref in enumerate(q_refs):

        @pl.when(piece == k)
        def _(q_ref=q_ref):
            for h in heads:
                q = q_ref[:, h * D : (h + 1) * D]
                qs[hr[h], :] = q
                scaled = q.astype(f32) * (SCALE * LOG2E)
                high = scaled.astype(bf16)
                qc[hr[h], :] = widened(high, (scaled - high.astype(f32)).astype(bf16))

    @pl.when(block == 0)
    def _():
        first = 0
        for ref in kv_refs:
            kv_ref[first : first + ref.shape[0], :] = ref[...]
            first += ref.shape[0]

    w = w_ref[...]

    kd = kv_ref[pl.ds(dbase, span), :D]
    vd = kv_ref[pl.ds(dbase, span), D:]
    vx = widened(vd)
    i_pos = start + lax.broadcasted_iota(jnp.int32, (rows, span), 0)
    j_pos = dbase + lax.broadcasted_iota(jnp.int32, (rows, span), 1)
    causal = j_pos <= i_pos
    far = j_pos < i_pos - WIN
    window = jnp.logical_and(causal, jnp.logical_not(far))
    xd = dot(w, kd, 1, 1).astype(bf16)
    phikd = key_features(xd, RATIO)
    s = dot(qc[...], widened(kd, kd), 1, 1)
    fqs = []
    for h in heads:
        x = dot(qs[hr[h], :], w[hw[h]], 1, 1).astype(bf16)
        e = jnp.exp(-jnp.abs(x))
        one = jnp.ones_like(x)
        fq = jnp.concatenate([jnp.where(x > 0, one + x, e), jnp.where(x > 0, e, one - x)], axis=1)
        fqs.append(fq * jnp.asarray(SIGMA, bf16))
        phiq[hr[h], :] = fqs[h]
    lins = [dot(fqs[h], phikd[hf[h]], 1, 0).astype(bf16) for h in heads]
    scs = [jnp.where(causal, s[hr[h]], big_negative) for h in heads]
    tops = [jnp.max(sc, axis=1, keepdims=True) for sc in scs]
    sws = [jnp.where(window, s[hr[h]], big_negative) for h in heads]
    peaks = [jnp.max(sw, axis=1, keepdims=True) for sw in sws]
    for h in heads:
        m_ref[hr[h], :] = jnp.broadcast_to(tops[h], (rows, D))
    ps = [jnp.exp2(scs[h] - tops[h]).astype(bf16) for h in heads]
    mixes = [jnp.where(far, lins[h], jnp.exp2(sws[h] - peaks[h]).astype(bf16)) for h in heads]
    acc[...] = dot(jnp.concatenate(ps, axis=0), vx, 1, 0)
    den[...] = dot(jnp.concatenate(mixes, axis=0), vx, 1, 0)

    def teacher_step(j0, n):
        kc = kv_ref[pl.ds(j0, n), :D]
        kk = widened(kc, kc)
        vc = widened(kv_ref[pl.ds(j0, n), D:])
        size = RATIO * rows // 4
        cuts = [slice(i * size, (i + 1) * size) for i in range(4)]
        scores = [dot(qc[c, :], kk, 1, 1) for c in cuts]
        for c, s in zip(cuts, scores):
            old = m_ref[c, :]
            new = jnp.maximum(old, jnp.max(s, axis=1, keepdims=True))
            m_ref[c, :] = new
            a = jnp.exp2(old - new)
            p = jnp.exp2(s - jnp.concatenate([new] * (n // D), axis=1)).astype(bf16)
            acc[c, :] = acc[c, :] * jnp.concatenate([a, a], axis=1) + dot(p, vc, 1, 0)

    def sweep(step, stop):
        def body(t, c):
            step(pl.multiple_of(low + t * most * rows, rows), most * rows)
            return c

        lax.fori_loop(0, (stop - low) // (most * rows), body, 0)
        size = most // 2
        while size:
            left = (stop - low) % (2 * size * rows)
            more = left >= size * rows
            if most >= 8 and size <= 2:
                last = (stop - low) % (4 * rows)
                more = jnp.logical_and(more, last != 3 * rows)
                if size == 2:

                    @pl.when(last == 3 * rows)
                    def _(last=last):
                        step(pl.multiple_of(stop - last, rows), 3 * rows)

            @pl.when(more)
            def _(size=size, left=left):
                step(pl.multiple_of(stop - left, rows), size * rows)

            size //= 2

    sweep(teacher_step, dbase)


def far_kernel(blocks, pieces, most, where_ref, *refs):
    n_in = blocks + 5 + pieces
    q_refs, (w_ref, m_in, acc_in, den, phiq, *kv_refs), err_refs, (out_ref, *scratch) = (
        refs[:blocks],
        refs[blocks:n_in],
        refs[n_in : n_in + blocks],
        refs[n_in + blocks :],
    )
    (kv_ref, errs, gw_ref, square, qs, qc, m_ref, acc, state, lsum, lx, xs) = scratch
    rows = q_refs[0].shape[0]
    D = HEAD_SIZE
    block = pl.program_id(0)
    piece = where_ref[2] ^ block
    low = pl.multiple_of(where_ref[1], rows)

    def reach(b):
        return pl.multiple_of(jnp.maximum(where_ref[0] + (b - 1) * rows, low), rows)

    start = where_ref[0] + block * rows
    dbase = reach(block)
    span = 2 * rows
    heads = range(RATIO)
    hr = [slice(h * rows, (h + 1) * rows) for h in heads]
    hf = [slice(h * 2 * FM, (h + 1) * 2 * FM) for h in heads]
    hw = [slice(h * FM, (h + 1) * FM) for h in heads]

    for k, q_ref in enumerate(q_refs):

        @pl.when(piece == k)
        def _(q_ref=q_ref):
            for h in heads:
                q = q_ref[:, h * D : (h + 1) * D]
                qs[hr[h], :] = q
                scaled = q.astype(f32) * (SCALE * LOG2E)
                high = scaled.astype(bf16)
                qc[hr[h], :] = widened(high, (scaled - high.astype(f32)).astype(bf16))

    @pl.when(block == 0)
    def _():
        first = 0
        for ref in kv_refs:
            kv_ref[first : first + ref.shape[0], :] = ref[...]
            first += ref.shape[0]

    w = w_ref[...]
    m_ref[...] = m_in[...]
    acc[...] = acc_in[...]

    kd = kv_ref[pl.ds(dbase, span), :D]
    vd = kv_ref[pl.ds(dbase, span), D:]
    vx = widened(vd)
    i_pos = start + lax.broadcasted_iota(jnp.int32, (rows, span), 0)
    j_pos = dbase + lax.broadcasted_iota(jnp.int32, (rows, span), 1)
    causal = j_pos <= i_pos
    far = j_pos < i_pos - WIN
    window = jnp.logical_and(causal, jnp.logical_not(far))
    xd = dot(w, kd, 1, 1).astype(bf16)
    phikd = key_features(xd, RATIO)

    def teacher_step(j0, n):
        kc = kv_ref[pl.ds(j0, n), :D]
        kk = widened(kc, kc)
        vc = widened(kv_ref[pl.ds(j0, n), D:])
        size = RATIO * rows // 4
        cuts = [slice(i * size, (i + 1) * size) for i in range(4)]
        scores = [dot(qc[c, :], kk, 1, 1) for c in cuts]
        for c, s in zip(cuts, scores):
            old = m_ref[c, :]
            new = jnp.maximum(old, jnp.max(s, axis=1, keepdims=True))
            m_ref[c, :] = new
            a = jnp.exp2(old - new)
            p = jnp.exp2(s - jnp.concatenate([new] * (n // D), axis=1)).astype(bf16)
            acc[c, :] = acc[c, :] * jnp.concatenate([a, a], axis=1) + dot(p, vc, 1, 0)

    def state_step(j0, n):
        kc = kv_ref[pl.ds(j0, n), :D]
        vc = widened(kv_ref[pl.ds(j0, n), D:])
        size = RATIO // 2
        xps = [dot(w[i * size * FM : (i + 1) * size * FM], kc, 1, 1).astype(bf16) for i in range(2)]
        for i, x in enumerate(xps):
            xs[i * size * FM : (i + 1) * size * FM, pl.ds(j0, n)] = x
            c = slice(i * size * 2 * FM, (i + 1) * size * 2 * FM)
            state[c, :] += dot(key_features(x, size), vc, 1, 0)

    def sweep(step, stop):
        def body(t, c):
            step(pl.multiple_of(low + t * most * rows, rows), most * rows)
            return c

        lax.fori_loop(0, (stop - low) // (most * rows), body, 0)
        size = most // 2
        while size:
            left = (stop - low) % (2 * size * rows)
            more = left >= size * rows
            if most >= 8 and size <= 2:
                last = (stop - low) % (4 * rows)
                more = jnp.logical_and(more, last != 3 * rows)
                if size == 2:

                    @pl.when(last == 3 * rows)
                    def _(last=last):
                        step(pl.multiple_of(stop - last, rows), 3 * rows)

            @pl.when(more)
            def _(size=size, left=left):
                step(pl.multiple_of(stop - left, rows), size * rows)

            size //= 2

    sweep(teacher_step, reach(0))

    @pl.when(block == 0)
    def _():
        state[...] = jnp.zeros_like(state)
        gw_ref[...] = jnp.zeros_like(gw_ref)
        square[...] = jnp.zeros_like(square)
        sweep(state_step, dbase)

    @pl.when(jnp.logical_and(block > 0, dbase > reach(block - 1)))
    def _():
        state_step(pl.multiple_of(dbase - rows, rows), rows)

    lane = lax.broadcasted_iota(jnp.int32, (rows, D), 1)
    lanef = lax.broadcasted_iota(jnp.int32, (2 * FM, D), 1)
    total = jnp.zeros((8, D), f32)
    gxs, sxs, firsts = [], [], []
    for h in heads:
        st = state[hf[h], :]
        sb = st[:, :D].astype(bf16)
        n = st[:, D:]
        n_hi = n.astype(bf16)
        n_lo = n - n_hi.astype(f32)
        firsts.append(dot(phiq[hr[h], :], widened(sb, n_hi), 1, 0))
        sxs.append(widened(sb, jnp.where(lanef == 2, n_lo, n).astype(bf16)))
    for h in heads:
        nd = den[hr[h], :] + firsts[h]
        inverse = 1.0 / nd[:, D:]
        student = nd[:, :D] * inverse
        teacher = acc[hr[h], :D] / acc[hr[h], D:]
        e = student - teacher
        errs[:, h * D : (h + 1) * D] = e.astype(errs.dtype)
        e2 = e * e
        for b in range(rows // 8):
            total = total + e2[b * 8 : (b + 1) * 8]
        go = (2.0 * e * inverse).astype(bf16)
        gd = -jnp.sum(go.astype(f32) * student, axis=1, keepdims=True)
        gd_hi = gd.astype(bf16).astype(f32)
        gdx = jnp.where(lane == 1, gd - gd_hi, jnp.where(lane <= 2, gd_hi, 0.0)).astype(bf16)
        gxs.append(widened(go, gdx))
    square[...] += total
    for k, err_ref in enumerate(err_refs):

        @pl.when(piece == k)
        def _(err_ref=err_ref):
            err_ref[...] = errs[...]

    gx = jnp.concatenate(gxs, axis=0)
    laned = lax.broadcasted_iota(jnp.int32, (span, D), 1)
    vg = widened(vd, jnp.where(laned == 2, 0.0, 1.0).astype(bf16))
    glin = dot(gx, vg, 1, 1)
    xqs = [dot(w[hw[h]], qs[hr[h], :], 1, 1).astype(bf16) for h in heads]
    fqts = [key_features(x, 1) * jnp.asarray(SIGMA, bf16) for x in xqs]
    gls = [jnp.where(far, glin[hr[h]], 0.0).astype(bf16) for h in heads]
    gouts = [dot(fqts[h], gls[h], 1, 0) for h in heads]
    gqs = [dot(sxs[h], gxs[h], 1, 1) + dot(phikd[hf[h]], gls[h], 1, 1) for h in heads]
    for h in heads:
        lsum[block, hf[h], :] = dot(fqts[h], gxs[h], 1, 0)
    ys = [(key_slopes(xqs[h], gqs[h], 1) * SIGMA).astype(bf16) for h in heads]
    for h in heads:
        gw_ref[hw[h], :] += dot(ys[h], qs[hr[h], :], 1, 0)
    gp = key_slopes(xd, jnp.concatenate(gouts, axis=0), RATIO).astype(bf16)
    gw_ref[...] += dot(gp, kd, 1, 0)

    def back_step(j0, n):
        kc = kv_ref[pl.ds(j0, n), :D]
        vc = widened(kv_ref[pl.ds(j0, n), D:])
        size = RATIO // 2
        gs = [dot(lx[i * size * 2 * FM : (i + 1) * size * 2 * FM, :], vc, 1, 1) for i in range(2)]
        for i, g in enumerate(gs):
            c = slice(i * size * FM, (i + 1) * size * FM)
            gw_ref[c, :] += dot(key_slopes(xs[c, pl.ds(j0, n)], g, size).astype(bf16), kc, 1, 0)

    @pl.when(block == blocks - 1)
    def _():
        for b in reversed(range(blocks)):
            if b < blocks - 1:
                lsum[b] += lsum[b + 1]
            l = lsum[b]
            lanel = lax.broadcasted_iota(jnp.int32, (l.shape[0], D), 1)
            ln = jnp.sum(jnp.where(lanel < 2, l[:, D:], 0.0), axis=1, keepdims=True)
            ln_hi = ln.astype(bf16).astype(f32)
            ln = jnp.where(lanel == 0, ln_hi, jnp.where(lanel == 1, ln - ln_hi, 0.0))
            lx[...] = widened(l[:, :D].astype(bf16), ln.astype(bf16))
            if b == 0:
                sweep(back_step, reach(0))
            else:
                here = reach(b)

                @pl.when(here > reach(b - 1))
                def _():
                    back_step(pl.multiple_of(here - rows, rows), rows)

        out_ref[: RATIO * FM, :] = gw_ref[...].astype(out_ref.dtype)
        row = lax.broadcasted_iota(jnp.int32, (TAIL, D), 0)
        rest = jnp.broadcast_to(jnp.sum(square[...], keepdims=True), (TAIL, D))
        tail = jnp.zeros((TAIL, D), f32)
        for k in range(3):
            part = rest.astype(out_ref.dtype).astype(f32)
            tail = jnp.where(row == k, part, tail)
            rest = rest - part
        out_ref[RATIO * FM :, :] = tail.astype(out_ref.dtype)


def attend(near, where, queries, weights_t, kv_near, kv, out_type):
    blocks = len(queries)
    rows, width = queries[0].shape
    D = HEAD_SIZE
    R = RATIO * rows
    F = RATIO * 2 * FM

    def all_of(shape):
        return pl.BlockSpec(shape, lambda b, p: (0, 0), pipeline_mode=pl.Buffered(1))

    def each(a):
        return pl.BlockSpec((pl.Squeezed(), *a.shape[1:]), lambda b, p: (b, 0, 0))

    def call(body, name, place, pieces, more, out_shape, out_specs, scratch, keys, most):
        return pl.pallas_call(
            functools.partial(body, blocks, len(pieces), most),
            name=name,
            out_shape=out_shape,
            grid_spec=pltpu.PrefetchScalarGridSpec(
                num_scalar_prefetch=1,
                grid=(blocks,),
                in_specs=[all_of((rows, width))] * blocks
                + [all_of((RATIO * FM, D))]
                + [each(a) for a in more]
                + [all_of(a.shape) for a in pieces],
                out_specs=out_specs,
                scratch_shapes=scratch,
            ),
            compiler_params=pltpu.CompilerParams(
                dimension_semantics=("arbitrary",), vmem_limit_bytes=56 << 20
            ),
            cost_estimate=pl.CostEstimate(
                flops=blocks * R * keys * D * 6,
                bytes_accessed=keys * 4 * D + R * blocks * D * 4,
                transcendentals=blocks * R * keys,
            ),
        )(place, *queries, weights_t, *more, *pieces)

    sums = [
        jax.ShapeDtypeStruct((blocks, R, D), f32),
        jax.ShapeDtypeStruct((blocks, R, 2 * D), f32),
        jax.ShapeDtypeStruct((blocks, R, 2 * D), f32),
        jax.ShapeDtypeStruct((blocks, R, 2 * FM), bf16),
    ]
    tokens = sum(a.shape[0] for a in kv_near)
    sums = call(
        near_kernel, "near", near, kv_near, [], sums, [each(a) for a in sums],
        [
            pltpu.VMEM((tokens, 2 * D), bf16),
            pltpu.VMEM((R, D), bf16),
            pltpu.VMEM((R, 2 * D), bf16),
        ],
        tokens, 2 if blocks > 2 else 1,
    )
    tokens = sum(a.shape[0] for a in kv)
    *error, gw = call(
        far_kernel, "far", where, kv, sums,
        [jax.ShapeDtypeStruct((rows, width), out_type)] * blocks
        + [jax.ShapeDtypeStruct((RATIO * FM + TAIL, D), out_type)],
        [all_of((rows, width))] * blocks + [all_of((RATIO * FM + TAIL, D))],
        [
            pltpu.VMEM((tokens, 2 * D), bf16),
            pltpu.VMEM((rows, width), out_type),
            pltpu.VMEM((RATIO * FM, D), f32),
            pltpu.VMEM((8, D), f32),
            pltpu.VMEM((R, D), bf16),
            pltpu.VMEM((R, 2 * D), bf16),
            pltpu.VMEM((R, D), f32),
            pltpu.VMEM((R, 2 * D), f32),
            pltpu.VMEM((F, 2 * D), f32),
            pltpu.VMEM((blocks, F, 2 * D), f32),
            pltpu.VMEM((F, 2 * D), bf16),
            pltpu.VMEM((RATIO * FM, tokens), bf16),
        ],
        tokens, 8,
    )
    return error, gw


def exchange(parts, ctx, unit):
    return [
        part if s == 0 else lax.ppermute(part, "ctx", [(i, i ^ (s * unit)) for i in range(ctx)])
        for s, part in enumerate(parts)
    ]


def pairwise(parts):
    while len(parts) > 1:
        parts = [parts[i] + parts[i + 1] for i in range(0, len(parts), 2)]
    return parts[0]


def in_order(parts, number):
    bit = 1
    while bit < len(parts):
        odd = (number & bit) > 0
        parts = [jnp.where(odd, parts[i ^ bit], parts[i]) for i in range(len(parts))]
        bit *= 2
    return parts


def shards(queries, keys, values, feature_weights):
    rows = queries.shape[0]
    heads = feature_weights.shape[0]
    groups = heads // RATIO
    D = HEAD_SIZE
    width = RATIO * D
    ctx = lax.axis_size("ctx")
    place = lax.axis_index("ctx")
    whole = rows * ctx * QUERY_HEADS
    weights_t = jnp.transpose(feature_weights, (0, 2, 1)).reshape(heads * FM, D)
    split = groups > 1 and groups & (groups - 1) == 0 and ctx in (2 * groups, 4 * groups)
    if not split:
        everything = lax.all_gather(jnp.concatenate([keys, values], axis=1), "ctx", axis=0, tiled=True)
        where = jnp.stack([place * rows, 0, 0]).astype(jnp.int32)
        near = jnp.stack([rows, jnp.where(place > 0, 0, rows), 0]).astype(jnp.int32)
        done = []
        for g in range(groups):
            kv = jnp.concatenate(
                [everything[:, g * D : (g + 1) * D], everything[:, (groups + g) * D : (groups + g + 1) * D]], axis=1
            )
            mine = jnp.concatenate([keys[:, g * D : (g + 1) * D], values[:, g * D : (g + 1) * D]], axis=1)
            before = lax.dynamic_slice_in_dim(kv, jnp.maximum(place - 1, 0) * rows, rows, 0)
            done.append(
                attend(near, where, [queries[:, g * width : (g + 1) * width]],
                       weights_t[g * RATIO * FM : (g + 1) * RATIO * FM], [before, mine, before], [kv], f32)
            )
        error = jnp.concatenate([d[0][0] for d in done], axis=1)
        cut = RATIO * FM
        loss = lax.psum(sum(jnp.sum(d[1][cut:, 0]) for d in done), ("ctx", "head")) / whole
        gw = lax.psum(jnp.concatenate([d[1][:cut] for d in done], axis=0), "ctx")
        return (error, loss, jnp.transpose(gw.reshape(heads, FM, D), (0, 2, 1)))

    slices = ctx // groups
    number = place % groups
    here = place // groups

    def of_group(a, s, n):
        return lax.dynamic_slice_in_dim(a, (number ^ s) * n, n, 1)

    members = range(groups)
    kv_parts = [jnp.concatenate([of_group(keys, s, D), of_group(values, s, D)], axis=1) for s in members]
    own = jnp.concatenate(in_order(exchange(kv_parts, ctx, 1), number), axis=0)
    before = lax.ppermute(own[-rows:], "ctx", [(i, i + groups) for i in range(ctx - groups)])
    q = exchange([of_group(queries, s, width) for s in members], ctx, 1)
    earlier = [
        lax.ppermute(own, "ctx", [(i, i + s * groups) for i in range(ctx - s * groups)])
        for s in range(1, slices)
    ]
    kv = earlier[::-1] + [own]
    run = groups * rows
    where = jnp.stack([(slices - 1) * run, (slices - 1 - here) * run, number]).astype(jnp.int32)
    near = jnp.stack([rows, jnp.where(here > 0, 0, rows), number]).astype(jnp.int32)
    w = lax.dynamic_slice_in_dim(weights_t, number * RATIO * FM, RATIO * FM, 0)
    error, gw = attend(near, where, q, w, [before, own], kv, bf16)
    back = in_order(exchange(error, ctx, 1), number)
    attn_error = jnp.concatenate(back, axis=1).astype(f32)
    gw = pairwise([a.astype(f32) for a in exchange([gw] * slices, ctx, groups)])
    cut = RATIO * FM
    rest = gw[cut] + gw[cut + 1] + gw[cut + 2]
    tail = []
    for k in range(3):
        tail.append(lax.reduce_precision(rest, 8, 7))
        rest = rest - tail[-1]
    tail = jnp.stack(tail + [jnp.zeros_like(rest)] * (TAIL - 3))
    parts = exchange([jnp.concatenate([gw[:cut], tail]).astype(bf16)] * groups, ctx, 1)
    tails = [p[cut : cut + 3].astype(f32) for p in parts]
    square = pairwise([a[0] + a[1] + a[2] for a in tails])
    count = lax.axis_size("head")
    if count == 2:
        square = square + lax.ppermute(square, "head", [(0, 1), (1, 0)])
    else:
        square = lax.psum(square, "head")
    square = square[0]
    gw = jnp.concatenate(in_order([p[:cut] for p in parts], number), axis=0).astype(f32)
    return (attn_error, square / whole, jnp.transpose(gw.reshape(heads, FM, D), (0, 2, 1)))


def solution(mesh):
    placed = (P("ctx", "head"), P("ctx", "head"), P("ctx", "head"), P("head", None, None))
    return jax.shard_map(
        shards,
        mesh=mesh,
        in_specs=placed,
        out_specs=(P("ctx", "head"), P(), P("head", None, None)),
        check_vma=False,
    )
```
